32 devices in a mesh: tok: 2 (over x), blk: 16 (over z, y, core).
Axes of the slice: x: 2, y: 2, z: 4, core: 2. Of those that a mesh axis runs over, the one named last changes fastest.
Arguments:
- hidden_in: bfloat16 [16, 256, 1024], P('blk', 'tok'), may hold values from -22 to 22
- seg_ids: int32 [16, 256], P('blk'), may hold values from 0 to 3, never falling along the last dimension, each value on 1 to 128 neighbouring positions
- norm_gain1: float32 [1024], replicated, may hold values from 0.1 to 1.9
- w_query: bfloat16 [1024, 1024], replicated, may hold values from -0.0234375 to 0.0234375
- w_key_value: bfloat16 [1024, 2048], replicated, may hold values from -0.1875 to 0.1875
- rel_bias: float32 [32, 16], replicated, may hold values from -3 to 300
- w_attn_out: bfloat16 [1024, 1024], replicated, may hold values from -0.1875 to 0.1875
- norm_gain2: float32 [1024], replicated, may hold values from 0.1 to 1.9
- w_in: bfloat16 [4096, 1024], P('blk'), may hold values from -0.1875 to 0.1875
- w_out: bfloat16 [4096, 1024], P('blk'), may hold values from -0.09375 to 0.09375
Outputs:
- layer_out: bfloat16 [16, 256, 1024], P('blk', 'tok')
The draws below stay inside these ranges and needn't reach their ends.
Inputs may be any that keep to these rules, and one draw needn't show every extreme that they name: `seg_ids`: in each stream the segment numbers never fall; each of the 4 segments is a run of 1 to 128 tokens, one exactly 128 long.
All inputs are finite; a program needn't handle non-finite values.
Results may differ from the reference program's by a relative error of at most 0.007.
Values may be sent and summed in bfloat16 or wider, within the bound.
A program may use at most 192 MiB of HBM per device.

```python
import math
import jax
import jax.numpy as jnp
import numpy as np
from jax import lax

D = 1024
HEADS = 16
HD = 64
FF = 4096
BUCKETS = 32
SEGS = 4
SEQ = 256
STREAMS = 16
MOST_SEG = 128
N_BLK = 16


def draw_hidden_in(key, part):
    base_key = jax.random.fold_in(key, 11)
    row_key = jax.random.fold_in(key, 12)
    column_key = jax.random.fold_in(key, 13)
    shape = (STREAMS, SEQ, D)
    column_scale = jnp.exp(jax.random.uniform(column_key, (D,), jnp.float32, -1.15, 1.15))
    base = jax.random.truncated_normal(base_key, -3.0, 3.0, shape, jnp.float32)
    row_scale = jnp.exp(jax.random.uniform(row_key, (STREAMS, SEQ, 1), jnp.float32, -0.69, 0.69))
    return (base * row_scale * column_scale).astype(jnp.bfloat16)


def draw_rel_bias(key, part):
    base = jax.random.uniform(jax.random.fold_in(key, 21), (BUCKETS, HEADS), jnp.float32, -3.0, 3.0)
    return base


def steps_of(stream_key, extent, split, least, top_value):
    loudness, own = 1.0, jax.random.fold_in(stream_key, 6)
    for position, shards_of in split:
        heights = jnp.exp(jax.random.uniform(jax.random.fold_in(own, position), (shards_of,), jnp.float32, least / len(split), top_value / len(split)))
        loudness = loudness * jnp.repeat(heights, extent[position] // shards_of).reshape([-1 if axis == position else 1 for axis in range(len(extent))])
    return loudness


def split_up(number_of, total, bound, skew):
    weights = [(1 << 20) // math.isqrt(standing ** skew) + 1 for standing in range(2, number_of + 1)]
    spare, counts = total - bound - (number_of - 1), [1] * (number_of - 1)
    while spare > 0:
        candidates = [i for i in range(number_of - 1) if counts[i] < bound]
        pool, budget = sum([weights[i] for i in candidates]), spare
        for i in candidates:
            addition = min(bound - counts[i], max(1, budget * weights[i] // pool), spare)
            counts[i] = counts[i] + addition
            spare = spare - addition
    return np.array([bound] + counts)


def uneven_parts(rng, amount, total, most, slope):
    if amount == 2:
        one = jax.random.randint(rng, (), max(1, total - most), min(most, total - 1) + 1)
        return jnp.stack([one, total - one])
    sizes = jnp.asarray(split_up(amount, total, most, slope), jnp.int32)
    couples = (amount - 1) // 2
    giver, sink = sizes[1:1 + 2 * couples:2], sizes[2:2 + 2 * couples:2]
    room = jnp.minimum(giver - 1, most - sink)
    passed = jax.random.randint(jax.random.fold_in(rng, 1), (couples,), 0, 1 << 20) % (room + 1)
    sizes = sizes.at[1:1 + 2 * couples:2].set(giver - passed).at[2:2 + 2 * couples:2].set(sink + passed)
    return sizes[jax.random.permutation(jax.random.fold_in(rng, 2), amount)]


def gaussian(stream_key, shape, deviation, most, shards=(), held_as=jnp.bfloat16):
    level = steps_of(stream_key, shape, shards, -0.22, 0.18) if shards else 1.0
    entries = jax.random.normal(stream_key, shape, jnp.float32) * deviation * level
    return jnp.minimum(jnp.maximum(entries, -most), most).astype(held_as)


def setup_inputs(seed: int = 0) -> dict:
    keys = jax.random.split(jax.random.key(seed), 11)
    return {
        "hidden_in": draw_hidden_in(jax.random.fold_in(keys[10], 71), 0),
        "seg_ids": jax.vmap(lambda own: jnp.searchsorted(jnp.cumsum(uneven_parts(own, SEGS, SEQ, MOST_SEG, 2)), jnp.arange(SEQ), side="right"))(jax.random.split(keys[1], STREAMS)).reshape((STREAMS, SEQ)).astype(jnp.int32),
        "norm_gain1": jnp.clip(1.0 + 0.18 * jax.random.normal(keys[2], (D,), jnp.float32), 0.1, 1.9),
        "w_query": gaussian(keys[3], (D, D), (D * HD) ** -0.5, 0.0234375),
        "w_key_value": gaussian(keys[4], (D, 2 * D), D ** -0.5, 0.1875),
        "rel_bias": draw_rel_bias(jax.random.fold_in(keys[10], 71), 0),
        "w_attn_out": gaussian(keys[6], (D, D), D ** -0.5, 0.1875),
        "norm_gain2": jnp.clip(1.0 + 0.18 * jax.random.normal(keys[7], (D,), jnp.float32), 0.1, 1.9),
        "w_in": gaussian(keys[8], (FF, D), D ** -0.5, 0.1875, ((0, 16),)),
        "w_out": gaussian(keys[9], (FF, D), FF ** -0.5, 0.09375, ((0, 16),)),
    }


bucket_bounds = (12, 16, 23, 32, 46, 64, 91)
epsilon = 1e-06

def bucket_of(offset):
    distance = jnp.abs(offset)
    far_bucket = jnp.full_like(distance, 8)
    for boundary in bucket_bounds:
        far_bucket = far_bucket + (distance >= boundary).astype(jnp.int32)
    chosen = jnp.where(distance < 8, distance, far_bucket)
    return chosen + 16 * (offset > 0).astype(jnp.int32)

def rms_scale(values, gain):
    mean_square = lax.optimization_barrier(jnp.mean(values * values, axis=-1, keepdims=True))
    return values * lax.rsqrt(mean_square + epsilon) * gain

def reference(hidden_in, seg_ids, norm_gain1, w_query, w_key_value, rel_bias, w_attn_out, norm_gain2, w_in, w_out):
    positions = jnp.arange(SEQ, dtype=jnp.int32)
    bucket_grid = bucket_of(positions[None, :] - positions[:, None])
    bias_grid = jnp.take(jnp.transpose(rel_bias), bucket_grid, axis=1)
    slice_width = FF // N_BLK

    def one_stream(operands):
        stream_in, segment_row = operands
        hidden = stream_in.astype(jnp.float32)
        normed = rms_scale(hidden, norm_gain1).astype(jnp.bfloat16)
        queries = jnp.dot(normed, w_query, preferred_element_type=jnp.float32).astype(jnp.bfloat16).reshape(SEQ, HEADS, HD)
        keys_values = jnp.dot(normed, w_key_value, preferred_element_type=jnp.float32).astype(jnp.bfloat16)
        key_heads = keys_values[:, :D].reshape(SEQ, HEADS, HD)
        value_heads = keys_values[:, D:].reshape(SEQ, HEADS, HD)
        scores = jnp.einsum('qhd,khd->hqk', queries.astype(jnp.float32), key_heads.astype(jnp.float32)) + bias_grid
        same_segment = (segment_row[:, None] == segment_row[None, :])[None]
        masked = jnp.where(same_segment, scores, -1e+30)
        row_max = lax.optimization_barrier(jnp.max(masked, axis=-1, keepdims=True))
        exps = jnp.where(same_segment, jnp.exp(masked - row_max), 0.0)
        denominator = lax.optimization_barrier(jnp.sum(exps, axis=-1))
        weights = exps.astype(jnp.bfloat16)
        mixed = jnp.einsum('hqk,khd->hqd', weights.astype(jnp.float32), value_heads.astype(jnp.float32)) / denominator[..., None]
        attended = jnp.transpose(mixed, (1, 0, 2)).reshape(SEQ, D).astype(jnp.bfloat16)
        middle = hidden + jnp.dot(attended, w_attn_out, preferred_element_type=jnp.float32)
        normed_two = rms_scale(middle, norm_gain2).astype(jnp.bfloat16)
        inner = jax.nn.relu(lax.dot_general(normed_two, w_in, (((1,), (1,)), ((), ())), preferred_element_type=jnp.float32)).astype(jnp.bfloat16)
        inner_groups = inner.reshape(SEQ, N_BLK, slice_width).astype(jnp.float32)
        out_groups = w_out.reshape(N_BLK, slice_width, D).astype(jnp.float32)
        partials = jnp.einsum('sjf,jfd->jsd', inner_groups, out_groups).astype(jnp.bfloat16)
        partials = lax.optimization_barrier(partials)
        feed = lax.optimization_barrier(jnp.sum(partials.astype(jnp.float32), axis=0))
        return (middle + feed).astype(jnp.bfloat16)
    return lax.map(one_stream, (hidden_in, seg_ids))
```

```python
import functools

import jax
import jax.numpy as jnp
from jax import lax
from jax.experimental import pallas as pl
from jax.experimental.pallas import tpu as pltpu
from jax.sharding import PartitionSpec as P

D = 1024
HEADS = 16
HD = 64
BUCKETS = 32

bucket_bounds = (12, 16, 23, 32, 46, 64, 91)
epsilon = 1e-06
MESH = pl.DeviceIdType.MESH
VM = pl.BlockSpec(memory_space=pltpu.VMEM)
HBM = pl.BlockSpec(memory_space=pltpu.HBM)
CUT = 4
AG = 2
BY_Z = ()


def bucket_of(offset):
    distance = jnp.abs(offset)
    far_bucket = jnp.full_like(distance, 8)
    for boundary in bucket_bounds:
        far_bucket = far_bucket + (distance >= boundary).astype(jnp.int32)
    chosen = jnp.where(distance < 8, distance, far_bucket)
    return chosen + 16 * (offset > 0).astype(jnp.int32)


def rms_scale(values, gain):
    mean_square = jnp.mean(values * values, axis=-1, keepdims=True)
    return values * lax.rsqrt(mean_square + epsilon) * gain


def layer_kernel(
    WIDE,
    x_hbm, seg_hbm, g1_hbm, bias_hbm, g2_hbm, wq_hbm, wkv_hbm, wo_hbm, win_hbm, wout_hbm, out_ref,
    seg, g1, bias, g2, wq, wkv, wo, win, wout, hid, q_scr, kv_scr, att_scr, mid, gath, part,
    inbox, inner_scr,
    s_load, s_hid, r_hid, s_pair, r_pair, s_far, s_near, r_w, s_hand, r_hand, s_z, s_y, s_on, r_gath,
    s_out, r_in,
):
    tok = lax.axis_index("tok")
    blk = lax.axis_index("blk")
    c = lax.rem(blk, 2)
    chip = blk // 2
    y = lax.rem(chip, WIDE)
    z = chip // WIDE
    zp = z + 1 - 2 * lax.rem(z, 2)
    zq = lax.rem(z + 2, 4)
    oc = 1 - c
    n_tok, rows, _ = hid.shape
    units = win.shape[1]
    piece = units // n_tok
    cols = wout.shape[3]
    slots = 2 * WIDE
    n_in = 2 if piece % 32 == 0 else 1
    n_piece = n_in + CUT

    def dev(zz, yy, cc):
        return {"blk": (zz * WIDE + yy) * 2 + cc}

    def beside(d):
        return lax.rem(y + d, WIDE)

    def other_tok(d):
        return lax.rem(tok + d, n_tok)

    def remote(src, dst, ss, rs, to):
        return pltpu.make_async_remote_copy(
            src_ref=src, dst_ref=dst, send_sem=ss, recv_sem=rs, device_id=to, device_id_type=MESH
        )

    sides = range(1, WIDE)
    toks = range(1, n_tok)
    core_dev = dev(z, y, oc)
    near_dev = dev(zp, y, c)
    far_dev = dev(zq, y, c)

    barrier = pltpu.get_barrier_semaphore()
    greet = [core_dev, near_dev, far_dev]
    greet += [dev(z, beside(d), c) for d in sides] + [{"tok": other_tok(d)} for d in toks]
    for to in greet:
        pl.semaphore_signal(barrier, inc=1, device_id=to, device_id_type=MESH)

    wanted = [
        (x_hbm, hid.at[tok]), (g1_hbm, g1), (wq_hbm, wq), (seg_hbm, seg), (bias_hbm, bias),
        (wkv_hbm, wkv), (wo_hbm, wo), (g2_hbm, g2), (win_hbm, win.at[0]),
    ]
    wanted += [(wout_hbm.at[:, j * cols:(j + 1) * cols], wout.at[j, 0]) for j in range(CUT)]
    loads = [pltpu.make_async_copy(src, dst, s_load.at[k]) for k, (src, dst) in enumerate(wanted)]
    for load in loads:
        load.start()
    pl.semaphore_wait(barrier, len(greet))

    hid_copies = [
        remote(x_hbm, hid.at[tok], s_hid.at[d], r_hid.at[d], {"tok": other_tok(d)}) for d in toks
    ]
    for copy in hid_copies:
        copy.start()

    def ends(p, d):
        base = lax.rem(tok + n_tok - d, n_tok) * piece
        if p < n_in:
            size = piece // n_in
            spot = pl.ds(pl.multiple_of(base + p * size, size), size)
            return win_hbm.at[spot], win.at[2, spot], win.at[3, spot]
        spot = pl.ds(pl.multiple_of(base, piece), piece)
        j = p - n_in
        return wout.at[j, 0, spot], wout.at[j, 2, spot], wout.at[j, 3, spot]

    def far_copy(p):
        src, dst, _ = ends(p, 0)
        return remote(src, dst, s_far.at[p], r_w.at[p, 0], far_dev)

    def relay(p, d):
        spot = ends(p, 0)[1]
        return remote(spot, spot, s_near.at[p, d], r_w.at[p, d], {"tok": other_tok(d)})

    def hand_copy(p, d):
        _, src, dst = ends(p, d)
        return remote(src, dst, s_hand.at[p, d], r_hand.at[p, d], core_dev)

    def pair_copy(k):
        src, dst = (win_hbm, win.at[1]) if k == 0 else (wout.at[k - 1, 0], wout.at[k - 1, 1])
        return remote(src, dst, s_pair.at[k], r_pair.at[k], core_dev)

    def share(p):
        far_copy(p).wait_recv()
        for d in toks:
            relay(p, d).start()
        hand_copy(p, 0).start()

    def hand(p):
        for d in toks:
            relay(p, d).wait_recv()
            hand_copy(p, d).start()

    def have(p):
        for d in range(n_tok):
            hand_copy(p, d).wait_recv()

    for p in range(n_in):
        far_copy(p).start()
    pair_copy(0).start()

    loads[0].wait()
    loads[1].wait()
    normed = rms_scale(hid[tok].astype(jnp.float32), g1[...]).astype(jnp.bfloat16)
    loads[2].wait()
    q_scr[...] = jnp.dot(normed, wq[...], preferred_element_type=jnp.float32).astype(jnp.bfloat16)
    loads[3].wait()
    loads[4].wait()
    loads[5].wait()

    def keys_values(values, who):
        kv_scr[pl.ds(pl.multiple_of(who * rows, rows), rows), :] = jnp.dot(
            values, wkv[...], preferred_element_type=jnp.float32
        ).astype(jnp.bfloat16)

    def seg_of(who):
        at = pl.ds(pl.multiple_of(who * rows, rows), rows)
        return jnp.broadcast_to(seg[:, at].astype(jnp.float32), (rows, rows))

    diagonal = lax.broadcasted_iota(jnp.int32, (rows, rows), 0) == (
        lax.broadcasted_iota(jnp.int32, (rows, rows), 1)
    )
    own_seg = jnp.sum(jnp.where(diagonal, seg_of(tok), 0.0), axis=-1, keepdims=True)
    low = lax.broadcasted_iota(jnp.int32, (rows, 2 * HD), 1) < HD
    zero = jnp.zeros((rows, 2 * HD), jnp.bfloat16)

    def both(values):
        return jnp.concatenate([jnp.where(low, values, zero), jnp.where(low, zero, values)], axis=0)

    def lines_of(who):
        spot = lax.broadcasted_iota(jnp.int32, (BUCKETS, 2 * rows), 1)
        offset = jnp.where(spot < rows, spot, spot - 2 * rows) + (who - tok) * rows
        chosen = lax.broadcasted_iota(jnp.int32, (BUCKETS, 2 * rows), 0) == bucket_of(offset)
        return jnp.dot(
            bias[...], chosen.astype(jnp.float32),
            precision=lax.Precision.HIGHEST, preferred_element_type=jnp.float32,
        )

    def attend(who, lines, same, state):
        held = pl.ds(pl.multiple_of(who * rows, rows), rows)
        found = []
        for pair in range(HEADS // 2):
            at = pair * 2 * HD
            scores = lax.dot_general(
                q_scr[:, at:at + 2 * HD], both(kv_scr[held, at:at + 2 * HD]),
                (((1,), (1,)), ((), ())), preferred_element_type=jnp.float32,
            )
            tops, totals, exps = [], [], []
            for half in range(2):
                head = 2 * pair + half
                line = jnp.broadcast_to(lines[head:head + 1, :], (rows, 2 * rows))
                shift = pltpu.roll(line, 0, 1, stride=1, stride_axis=0)[:, :rows]
                masked = jnp.where(same, scores[:, half * rows:(half + 1) * rows] + shift, -1e30)
                top = jnp.max(masked, axis=-1, keepdims=True)
                if state is not None:
                    top = jnp.maximum(top, state[pair][0][half])
                exp = jnp.exp(masked - top)
                tops.append(top)
                totals.append(jnp.sum(exp, axis=-1, keepdims=True))
                exps.append(exp.astype(jnp.bfloat16))
            mixed = jnp.dot(
                jnp.concatenate(exps, axis=1), both(kv_scr[held, D + at:D + at + 2 * HD]),
                preferred_element_type=jnp.float32,
            )
            if state is not None:
                old_tops, old_totals, old_mixed = state[pair]
                scale = [jnp.exp(old_tops[half] - tops[half]) for half in range(2)]
                totals = [totals[half] + scale[half] * old_totals[half] for half in range(2)]
                mixed = mixed + old_mixed * jnp.where(low, scale[0], scale[1])
            found.append((tops, totals, mixed))
        return found

    keys_values(normed, tok)
    state = attend(tok, lines_of(tok), own_seg == seg_of(tok), None)
    for d in toks:
        who = lax.rem(tok + n_tok - d, n_tok)
        lines = lines_of(who)
        same = own_seg == seg_of(who)
        hid_copies[d - 1].wait_recv()
        keys_values(rms_scale(hid[who].astype(jnp.float32), g1[...]).astype(jnp.bfloat16), who)
        if d == 1:
            for load in loads[6:]:
                load.wait()
            for k in range(CUT):
                pair_copy(k + 1).start()
            share(0)
        state = attend(who, lines, same, state)
    for pair, (_, totals, mixed) in enumerate(state):
        at = pair * 2 * HD
        att_scr[:, at:at + 2 * HD] = (mixed / jnp.where(low, totals[0], totals[1])).astype(
            jnp.bfloat16
        )
    middle = hid[tok].astype(jnp.float32) + jnp.dot(
        att_scr[...], wo[...], preferred_element_type=jnp.float32
    )
    mid[...] = middle
    gath[0] = rms_scale(middle, g2[...]).astype(jnp.bfloat16)

    ag_rows = rows // AG

    def rows_at(slot, h):
        return gath.at[slot, pl.ds(h * ag_rows, ag_rows)]

    def z_copy(h):
        return remote(rows_at(0, h), rows_at(WIDE, h), s_z.at[h], r_gath.at[WIDE, h], near_dev)

    def y_copy(d, h):
        slot = WIDE - d
        to = dev(z, beside(d), c)
        return remote(rows_at(0, h), rows_at(slot, h), s_y.at[d, h], r_gath.at[slot, h], to)

    def on_copy(d, h):
        if h in BY_Z:
            slot, to = WIDE + d, near_dev
            return remote(rows_at(d, h), rows_at(slot, h), s_on.at[d, h], r_gath.at[slot, h], to)
        slot, to = slots - d, dev(z, beside(d), c)
        return remote(rows_at(WIDE, h), rows_at(slot, h), s_on.at[d, h], r_gath.at[slot, h], to)

    def arrived(slot, h):
        remote(
            rows_at(slot, h), rows_at(slot, h), s_z.at[h], r_gath.at[slot, h], core_dev
        ).wait_recv()

    def first(lo, n, k, n_k):
        inner = lax.dot_general(
            gath[lo:lo + n].reshape(n * rows, D), win[k:k + n_k].reshape(n_k * units, D),
            (((1,), (1,)), ((), ())), preferred_element_type=jnp.float32,
        )
        inner_scr[lo * rows:(lo + n) * rows, k * units:(k + n_k) * units] = jnp.maximum(
            inner, 0.0
        ).astype(jnp.bfloat16)

    def second(j):
        terms = jnp.dot(
            inner_scr[...], wout[j].reshape(4 * units, cols), preferred_element_type=jnp.float32
        )
        at = slice(j * cols, (j + 1) * cols)
        mid[:, at] = mid[:, at] + terms[:rows]
        part[j] = terms.astype(jnp.bfloat16).reshape(slots, rows, cols)

    def send_sum(kind, d, slot, j, to):
        return remote(
            part.at[j, slot], inbox.at[kind, d, j], s_out.at[kind, d, j], r_in.at[kind, d, j], to
        )

    def corner_sum(d, j):
        to = dev(z, beside(d), c) if j % 2 == 0 else near_dev
        return send_sum(0, d, WIDE + d, j, to)

    def side_sum(d, j):
        return send_sum(1, d, d, j, dev(z, beside(d), c))

    def near_sum(j):
        return send_sum(2, 0, WIDE, j, near_dev)

    def got(kind, d, j):
        send_sum(kind, d, 0, j, core_dev).wait_recv()
        return inbox[kind, d, j].astype(jnp.float32)

    def send(j):
        for d in sides:
            corner_sum(d, j).start()
        if j % 2 == 0:
            for d in sides:
                side_sum(d, j).start()
        else:
            near_sum(j).start()

    def merge(j):
        if j % 2 == 0:
            extra = got(0, 1, j)
            for d in sides[1:]:
                extra = extra + got(0, d, j)
            part[j, WIDE] = (part[j, WIDE].astype(jnp.float32) + extra).astype(jnp.bfloat16)
            near_sum(j).start()
        else:
            for d in sides:
                part[j, d] = (part[j, d].astype(jnp.float32) + got(0, d, j)).astype(jnp.bfloat16)
                side_sum(d, j).start()

    for h in range(AG):
        z_copy(h).start()
        for d in sides:
            y_copy(d, h).start()
    for p in range(n_in, n_piece):
        far_copy(p).start()
    pair_copy(0).wait_recv()
    first(0, 1, 0, 2)
    for p in range(1, n_in):
        share(p)
    hand(0)
    for h in range(AG):
        if h in BY_Z:
            for d in sides:
                arrived(d, h)
                on_copy(d, h).start()
        else:
            arrived(WIDE, h)
            for d in sides:
                on_copy(d, h).start()
        if h == 0:
            for p in range(1, n_in):
                hand(p)
    for p in range(n_in):
        have(p)
    first(0, 1, 2, 2)
    for h in range(AG):
        if h in BY_Z:
            arrived(WIDE, h)
        else:
            for d in sides:
                arrived(d, h)
    first(1, WIDE, 0, 4)
    share(n_in)
    share(n_in + 1)
    hand(n_in)
    for d in sides:
        for h in range(AG):
            arrived(WIDE + d, h)
    first(WIDE + 1, WIDE - 1, 0, 4)
    for k in range(CUT):
        pair_copy(k + 1).wait_recv()
    hand(n_in + 1)
    for j in range(CUT):
        p = n_in + j
        if j > 1:
            hand(p)
        if j > 0 and p + 1 < n_piece:
            share(p + 1)
        if j > 1:
            merge(j - 2)
        have(p)
        second(j)
        send(j)
    for j in range(max(CUT - 2, 0), CUT):
        merge(j)
    for j in range(CUT):
        at = slice(j * cols, (j + 1) * cols)
        total = mid[:, at]
        for d in sides:
            total = total + got(1, d, j)
        total = total + got(2, 0, j)
        out_ref[:, at] = total.astype(jnp.bfloat16)

    for copy in hid_copies:
        copy.wait_send()
    for k in range(1 + CUT):
        pair_copy(k).wait_send()
    for p in range(n_piece):
        far_copy(p).wait_send()
        for d in toks:
            relay(p, d).wait_send()
        for d in range(n_tok):
            hand_copy(p, d).wait_send()
    for h in range(AG):
        z_copy(h).wait_send()
        for d in sides:
            y_copy(d, h).wait_send()
            on_copy(d, h).wait_send()
    for j in range(CUT):
        for d in sides:
            corner_sum(d, j).wait_send()
            side_sum(d, j).wait_send()
        near_sum(j).wait_send()


def per_device(
    n_tok, n_blk, hidden_in, seg_ids, norm_gain1, w_query, w_key_value, rel_bias, w_attn_out,
    norm_gain2, w_in, w_out,
):
    rows = hidden_in.shape[1]
    count = n_tok * rows
    units = w_in.shape[0]
    wide = n_blk // 8
    chips = 2 * wide
    cols = D // CUT
    dma = pltpu.SemaphoreType.DMA

    def half(*shape):
        return pltpu.VMEM(shape, jnp.bfloat16)

    def full(*shape):
        return pltpu.VMEM(shape, jnp.float32)

    out = pl.pallas_call(
        functools.partial(layer_kernel, wide),
        out_shape=jax.ShapeDtypeStruct((rows, D), jnp.bfloat16),
        in_specs=[HBM] * 10,
        out_specs=VM,
        scratch_shapes=[
            pltpu.VMEM((1, count), jnp.int32),
            full(1, D),
            full(HEADS, BUCKETS),
            full(1, D),
            half(D, D),
            half(D, 2 * D),
            half(D, D),
            half(4, units, D),
            half(CUT, 4, units, cols),
            half(n_tok, rows, D),
            half(rows, D),
            half(count, 2 * D),
            half(rows, D),
            full(rows, D),
            half(chips, rows, D),
            half(CUT, chips, rows, cols),
            half(3, wide, CUT, rows, cols),
            half(chips * rows, 4 * units),
            dma((9 + CUT,)),
            dma((n_tok,)),
            dma((n_tok,)),
            dma((1 + CUT,)),
            dma((1 + CUT,)),
            dma((2 + CUT,)),
            dma((2 + CUT, n_tok)),
            dma((2 + CUT, n_tok)),
            dma((2 + CUT, n_tok)),
            dma((2 + CUT, n_tok)),
            dma((AG,)),
            dma((wide, AG)),
            dma((wide, AG)),
            dma((chips, AG)),
            dma((3, wide, CUT)),
            dma((3, wide, CUT)),
        ],
        compiler_params=pltpu.CompilerParams(
            collective_id=0, has_side_effects=True, vmem_limit_bytes=48 << 20
        ),
    )(
        *[
            pltpu.with_memory_space_constraint(operand, pltpu.HBM)
            for operand in (
                hidden_in[0], seg_ids, norm_gain1[None], jnp.transpose(rel_bias),
                norm_gain2[None], w_query, w_key_value, w_attn_out, w_in, w_out,
            )
        ]
    )
    return out[None]


def solution(mesh):
    placed = (
        P("blk", "tok", None),
        P("blk", None),
        P(),
        P(),
        P(),
        P(),
        P(),
        P(),
        P("blk", None),
        P("blk", None),
    )
    return jax.shard_map(
        functools.partial(per_device, mesh.shape["tok"], mesh.shape["blk"]),
        mesh=mesh, in_specs=placed, out_specs=P("blk", "tok", None), check_vma=False,
    )
```

```python
import functools

import jax
import jax.numpy as jnp
from jax import lax
from jax.experimental import pallas as pl
from jax.experimental.pallas import tpu as pltpu
from jax.sharding import PartitionSpec as P

D = 1024
HEADS = 16
HD = 64
BUCKETS = 32

bucket_bounds = (12, 16, 23, 32, 46, 64, 91)
epsilon = 1e-06
MESH = pl.DeviceIdType.MESH
VM = pl.BlockSpec(memory_space=pltpu.VMEM)
HBM = pl.BlockSpec(memory_space=pltpu.HBM)
CUT = 4
AG = 2
BY_Z = ()


def bucket_of(offset):
    distance = jnp.abs(offset)
    far_bucket = jnp.full_like(distance, 8)
    for boundary in bucket_bounds:
        far_bucket = far_bucket + (distance >= boundary).astype(jnp.int32)
    chosen = jnp.where(distance < 8, distance, far_bucket)
    return chosen + 16 * (offset > 0).astype(jnp.int32)


def rms_scale(values, gain):
    mean_square = jnp.mean(values * values, axis=-1, keepdims=True)
    return values * lax.rsqrt(mean_square + epsilon) * gain


def layer_kernel(
    WIDE,
    x_hbm, seg_hbm, g1_hbm, bias_hbm, g2_hbm, wq_hbm, wkv_hbm, wo_hbm, win_hbm, wout_hbm, out_ref,
    seg, g1, bias, g2, wq, wkv, wo, win, wout, hid, q_scr, kv_scr, att_scr, mid, gath, part,
    inbox, inner_scr,
    s_load, s_hid, r_hid, s_pair, r_pair, s_far, s_near, r_w, s_hand, r_hand, s_z, s_y, s_on, r_gath,
    s_out, r_in,
):
    tok = lax.axis_index("tok")
    blk = lax.axis_index("blk")
    c = lax.rem(blk, 2)
    chip = blk // 2
    y = lax.rem(chip, WIDE)
    z = chip // WIDE
    zp = z + 1 - 2 * lax.rem(z, 2)
    zq = 3 - z
    at_end = pl.when(lax.rem(z, 3) == 0)
    inside = pl.when(lax.rem(z, 3) != 0)
    oc = 1 - c
    n_tok, rows, _ = hid.shape
    units = win.shape[1]
    piece = units // n_tok
    cols = wout.shape[3]
    slots = 2 * WIDE
    n_in = 2 if piece % 32 == 0 else 1
    n_piece = n_in + CUT

    def dev(zz, yy, cc):
        return {"blk": (zz * WIDE + yy) * 2 + cc}

    def beside(d):
        return lax.rem(y + d, WIDE)

    def other_tok(d):
        return lax.rem(tok + d, n_tok)

    def remote(src, dst, ss, rs, to):
        return pltpu.make_async_remote_copy(
            src_ref=src, dst_ref=dst, send_sem=ss, recv_sem=rs, device_id=to, device_id_type=MESH
        )

    sides = range(1, WIDE)
    toks = range(1, n_tok)
    core_dev = dev(z, y, oc)
    near_dev = dev(zp, y, c)
    far_dev = dev(zq, y, c)

    barrier = pltpu.get_barrier_semaphore()
    greet = [core_dev, near_dev, far_dev]
    greet += [dev(z, beside(d), c) for d in sides] + [{"tok": other_tok(d)} for d in toks]
    for to in greet:
        pl.semaphore_signal(barrier, inc=1, device_id=to, device_id_type=MESH)

    wanted = [
        (x_hbm, hid.at[tok]), (g1_hbm, g1), (wq_hbm, wq), (seg_hbm, seg), (bias_hbm, bias),
        (wkv_hbm, wkv), (wo_hbm, wo), (g2_hbm, g2), (win_hbm, win.at[0]),
    ]
    wanted += [(wout_hbm.at[:, j * cols:(j + 1) * cols], wout.at[j, 0]) for j in range(CUT)]
    loads = [pltpu.make_async_copy(src, dst, s_load.at[k]) for k, (src, dst) in enumerate(wanted)]
    for load in loads:
        load.start()
    pl.semaphore_wait(barrier, len(greet))

    hid_copies = [
        remote(x_hbm, hid.at[tok], s_hid.at[d], r_hid.at[d], {"tok": other_tok(d)}) for d in toks
    ]
    for copy in hid_copies:
        copy.start()

    def ends(p, d):
        base = lax.rem(tok + n_tok - d, n_tok) * piece
        if p < n_in:
            size = piece // n_in
            spot = pl.ds(pl.multiple_of(base + p * size, size), size)
            return win_hbm.at[spot], win.at[2, spot], win.at[3, spot]
        spot = pl.ds(pl.multiple_of(base, piece), piece)
        j = p - n_in
        return wout.at[j, 0, spot], wout.at[j, 2, spot], wout.at[j, 3, spot]

    def far_copy(p):
        src, dst, _ = ends(p, 0)
        return remote(src, dst, s_far.at[p], r_w.at[p, 0], far_dev)

    def relay(p, d):
        spot = ends(p, 0)[1]
        return remote(spot, spot, s_near.at[p, d], r_w.at[p, d], {"tok": other_tok(d)})

    def hand_copy(p, d):
        _, src, dst = ends(p, d)
        return remote(src, dst, s_hand.at[p, d], r_hand.at[p, d], core_dev)

    def pair_copy(k):
        src, dst = (win_hbm, win.at[1]) if k == 0 else (wout.at[k - 1, 0], wout.at[k - 1, 1])
        return remote(src, dst, s_pair.at[k], r_pair.at[k], core_dev)

    def share(p):
        far_copy(p).wait_recv()
        for d in toks:
            relay(p, d).start()
        hand_copy(p, 0).start()

    def push(p, done):
        far_copy(done).wait_send()
        far_copy(p).start()

    def hand(p):
        for d in toks:
            relay(p, d).wait_recv()
            hand_copy(p, d).start()

    def have(p):
        for d in range(n_tok):
            hand_copy(p, d).wait_recv()

    for p in range(n_in):
        far_copy(p).start()
    pair_copy(0).start()

    loads[0].wait()
    loads[1].wait()
    normed = rms_scale(hid[tok].astype(jnp.float32), g1[...]).astype(jnp.bfloat16)
    loads[2].wait()
    q_scr[...] = jnp.dot(normed, wq[...], preferred_element_type=jnp.float32).astype(jnp.bfloat16)
    for load in loads[9:]:
        load.wait()
    for k in range(CUT):
        pair_copy(k + 1).start()
    loads[3].wait()
    loads[4].wait()
    loads[5].wait()

    def keys_values(values, who):
        kv_scr[pl.ds(pl.multiple_of(who * rows, rows), rows), :] = jnp.dot(
            values, wkv[...], preferred_element_type=jnp.float32
        ).astype(jnp.bfloat16)

    def seg_of(who):
        at = pl.ds(pl.multiple_of(who * rows, rows), rows)
        return jnp.broadcast_to(seg[:, at].astype(jnp.float32), (rows, rows))

    diagonal = lax.broadcasted_iota(jnp.int32, (rows, rows), 0) == (
        lax.broadcasted_iota(jnp.int32, (rows, rows), 1)
    )
    own_seg = jnp.sum(jnp.where(diagonal, seg_of(tok), 0.0), axis=-1, keepdims=True)
    low = lax.broadcasted_iota(jnp.int32, (rows, 2 * HD), 1) < HD
    zero = jnp.zeros((rows, 2 * HD), jnp.bfloat16)

    def both(values):
        return jnp.concatenate([jnp.where(low, values, zero), jnp.where(low, zero, values)], axis=0)

    def lines_of(who):
        spot = lax.broadcasted_iota(jnp.int32, (BUCKETS, 2 * rows), 1)
        offset = jnp.where(spot < rows, spot, spot - 2 * rows) + (who - tok) * rows
        chosen = lax.broadcasted_iota(jnp.int32, (BUCKETS, 2 * rows), 0) == bucket_of(offset)
        return jnp.dot(
            bias[...], chosen.astype(jnp.float32),
            precision=lax.Precision.HIGHEST, preferred_element_type=jnp.float32,
        )

    def attend(who, lines, same, state):
        held = pl.ds(pl.multiple_of(who * rows, rows), rows)
        found = []
        for pair in range(HEADS // 2):
            at = pair * 2 * HD
            scores = lax.dot_general(
                q_scr[:, at:at + 2 * HD], both(kv_scr[held, at:at + 2 * HD]),
                (((1,), (1,)), ((), ())), preferred_element_type=jnp.float32,
            )
            tops, totals, exps = [], [], []
            for half in range(2):
                head = 2 * pair + half
                line = jnp.broadcast_to(lines[head:head + 1, :], (rows, 2 * rows))
                shift = pltpu.roll(line, 0, 1, stride=1, stride_axis=0)[:, :rows]
                masked = jnp.where(same, scores[:, half * rows:(half + 1) * rows] + shift, -1e30)
                top = jnp.max(masked, axis=-1, keepdims=True)
                if state is not None:
                    top = jnp.maximum(top, state[pair][0][half])
                exp = jnp.exp(masked - top)
                tops.append(top)
                totals.append(jnp.sum(exp, axis=-1, keepdims=True))
                exps.append(exp.astype(jnp.bfloat16))
            mixed = jnp.dot(
                jnp.concatenate(exps, axis=1), both(kv_scr[held, D + at:D + at + 2 * HD]),
                preferred_element_type=jnp.float32,
            )
            if state is not None:
                old_tops, old_totals, old_mixed = state[pair]
                scale = [jnp.exp(old_tops[half] - tops[half]) for half in range(2)]
                totals = [totals[half] + scale[half] * old_totals[half] for half in range(2)]
                mixed = mixed + old_mixed * jnp.where(low, scale[0], scale[1])
            found.append((tops, totals, mixed))
        return found

    keys_values(normed, tok)
    state = attend(tok, lines_of(tok), own_seg == seg_of(tok), None)
    for d in toks:
        who = lax.rem(tok + n_tok - d, n_tok)
        lines = lines_of(who)
        same = own_seg == seg_of(who)
        if d == 1:
            @at_end
            def _():
                push(n_in, n_in - 1)

        hid_copies[d - 1].wait_recv()
        keys_values(rms_scale(hid[who].astype(jnp.float32), g1[...]).astype(jnp.bfloat16), who)
        if d == 1:
            for load in loads[6:9]:
                load.wait()
            at_end(lambda: share(0))
        state = attend(who, lines, same, state)
    for pair, (_, totals, mixed) in enumerate(state):
        at = pair * 2 * HD
        att_scr[:, at:at + 2 * HD] = (mixed / jnp.where(low, totals[0], totals[1])).astype(
            jnp.bfloat16
        )
    for p in range(1, n_in):
        at_end(functools.partial(share, p))
    middle = hid[tok].astype(jnp.float32) + jnp.dot(
        att_scr[...], wo[...], preferred_element_type=jnp.float32
    )
    mid[...] = middle
    gath[0] = rms_scale(middle, g2[...]).astype(jnp.bfloat16)

    ag_rows = rows // AG

    def rows_at(slot, h):
        return gath.at[slot, pl.ds(h * ag_rows, ag_rows)]

    def z_copy(h):
        return remote(rows_at(0, h), rows_at(WIDE, h), s_z.at[h], r_gath.at[WIDE, h], near_dev)

    def y_copy(d, h):
        slot = WIDE - d
        to = dev(z, beside(d), c)
        return remote(rows_at(0, h), rows_at(slot, h), s_y.at[d, h], r_gath.at[slot, h], to)

    def on_copy(d, h):
        if h in BY_Z:
            slot, to = WIDE + d, near_dev
            return remote(rows_at(d, h), rows_at(slot, h), s_on.at[d, h], r_gath.at[slot, h], to)
        slot, to = slots - d, dev(z, beside(d), c)
        return remote(rows_at(WIDE, h), rows_at(slot, h), s_on.at[d, h], r_gath.at[slot, h], to)

    def arrived(slot, h):
        remote(
            rows_at(slot, h), rows_at(slot, h), s_z.at[h], r_gath.at[slot, h], core_dev
        ).wait_recv()

    def first(lo, n, k, n_k):
        inner = lax.dot_general(
            gath[lo:lo + n].reshape(n * rows, D), win[k:k + n_k].reshape(n_k * units, D),
            (((1,), (1,)), ((), ())), preferred_element_type=jnp.float32,
        )
        inner_scr[lo * rows:(lo + n) * rows, k * units:(k + n_k) * units] = jnp.maximum(
            inner, 0.0
        ).astype(jnp.bfloat16)

    def second(j):
        terms = jnp.dot(
            inner_scr[...], wout[j].reshape(4 * units, cols), preferred_element_type=jnp.float32
        )
        at = slice(j * cols, (j + 1) * cols)
        mid[:, at] = mid[:, at] + terms[:rows]
        part[j] = terms.astype(jnp.bfloat16).reshape(slots, rows, cols)

    def send_sum(kind, d, slot, j, to):
        return remote(
            part.at[j, slot], inbox.at[kind, d, j], s_out.at[kind, d, j], r_in.at[kind, d, j], to
        )

    def corner_sum(d, j):
        to = dev(z, beside(d), c) if j % 2 == 0 else near_dev
        return send_sum(0, d, WIDE + d, j, to)

    def side_sum(d, j):
        return send_sum(1, d, d, j, dev(z, beside(d), c))

    def near_sum(j):
        return send_sum(2, 0, WIDE, j, near_dev)

    def got(kind, d, j):
        send_sum(kind, d, 0, j, core_dev).wait_recv()
        return inbox[kind, d, j].astype(jnp.float32)

    def send(j):
        for d in sides:
            corner_sum(d, j).start()
        if j % 2 == 0:
            for d in sides:
                side_sum(d, j).start()
        else:
            near_sum(j).start()

    def merge(j):
        if j % 2 == 0:
            extra = got(0, 1, j)
            for d in sides[1:]:
                extra = extra + got(0, d, j)
            part[j, WIDE] = (part[j, WIDE].astype(jnp.float32) + extra).astype(jnp.bfloat16)
            near_sum(j).start()
        else:
            for d in sides:
                part[j, d] = (part[j, d].astype(jnp.float32) + got(0, d, j)).astype(jnp.bfloat16)
                side_sum(d, j).start()

    for h in range(AG):
        z_copy(h).start()
        for d in sides:
            y_copy(d, h).start()
    w0, w1, w2, w3 = range(n_in, n_piece)

    @inside
    def _():
        push(w0, n_in - 1)
        far_copy(w1).start()

    pair_copy(0).wait_recv()
    first(0, 1, 0, 2)
    at_end(lambda: share(w0))

    def pass_on(h):
        if h in BY_Z:
            for d in sides:
                arrived(d, h)
                on_copy(d, h).start()
        else:
            arrived(WIDE, h)
            for d in sides:
                on_copy(d, h).start()

    for h in range(AG // 2):
        pass_on(h)

    @inside
    def _():
        for p in range(n_in):
            share(p)

    for h in range(AG // 2, AG):
        pass_on(h)

    @inside
    def _():
        push(w2, w0)
        push(w3, w1)
        share(w0)
        share(w1)

    @at_end
    def _():
        push(w1, w0)
        far_copy(w2).start()

    for p in range(n_in):
        hand(p)
    for h in range(AG):
        if h in BY_Z:
            arrived(WIDE, h)
        else:
            for d in sides:
                arrived(d, h)
    first(1, WIDE, 0, 2)

    @inside
    def _():
        share(w2)
        share(w3)

    for p in range(n_in):
        have(p)
    first(0, WIDE + 1, 2, 2)

    @at_end
    def _():
        push(w3, w1)
        share(w1)

    hand(w0)
    for d in sides:
        for h in range(AG):
            arrived(WIDE + d, h)
    first(WIDE + 1, WIDE - 1, 0, 4)
    for k in range(CUT):
        pair_copy(k + 1).wait_recv()
    have(w0)
    second(0)
    send(0)
    hand(w1)
    have(w1)
    second(1)
    send(1)
    at_end(lambda: share(w2))
    hand(w2)
    merge(0)
    have(w2)
    second(2)
    send(2)
    at_end(lambda: share(w3))
    hand(w3)
    merge(1)
    have(w3)
    second(3)
    send(3)
    merge(2)
    merge(3)
    for j in range(CUT):
        at = slice(j * cols, (j + 1) * cols)
        total = mid[:, at]
        for d in sides:
            total = total + got(1, d, j)
        total = total + got(2, 0, j)
        out_ref[:, at] = total.astype(jnp.bfloat16)

    for copy in hid_copies:
        copy.wait_send()
    for k in range(1 + CUT):
        pair_copy(k).wait_send()
    for p in (*range(n_in - 1), w2, w3):
        far_copy(p).wait_send()
    for p in range(n_piece):
        for d in toks:
            relay(p, d).wait_send()
        for d in range(n_tok):
            hand_copy(p, d).wait_send()
    for h in range(AG):
        z_copy(h).wait_send()
        for d in sides:
            y_copy(d, h).wait_send()
            on_copy(d, h).wait_send()
    for j in range(CUT):
        for d in sides:
            corner_sum(d, j).wait_send()
            side_sum(d, j).wait_send()
        near_sum(j).wait_send()


def per_device(
    n_tok, n_blk, hidden_in, seg_ids, norm_gain1, w_query, w_key_value, rel_bias, w_attn_out,
    norm_gain2, w_in, w_out,
):
    rows = hidden_in.shape[1]
    count = n_tok * rows
    units = w_in.shape[0]
    wide = n_blk // 8
    chips = 2 * wide
    cols = D // CUT
    dma = pltpu.SemaphoreType.DMA

    def half(*shape):
        return pltpu.VMEM(shape, jnp.bfloat16)

    def full(*shape):
        return pltpu.VMEM(shape, jnp.float32)

    out = pl.pallas_call(
        functools.partial(layer_kernel, wide),
        out_shape=jax.ShapeDtypeStruct((rows, D), jnp.bfloat16),
        in_specs=[HBM] * 10,
        out_specs=VM,
        scratch_shapes=[
            pltpu.VMEM((1, count), jnp.int32),
            full(1, D),
            full(HEADS, BUCKETS),
            full(1, D),
            half(D, D),
            half(D, 2 * D),
            half(D, D),
            half(4, units, D),
            half(CUT, 4, units, cols),
            half(n_tok, rows, D),
            half(rows, D),
            half(count, 2 * D),
            half(rows, D),
            full(rows, D),
            half(chips, rows, D),
            half(CUT, chips, rows, cols),
            half(3, wide, CUT, rows, cols),
            half(chips * rows, 4 * units),
            dma((9 + CUT,)),
            dma((n_tok,)),
            dma((n_tok,)),
            dma((1 + CUT,)),
            dma((1 + CUT,)),
            dma((2 + CUT,)),
            dma((2 + CUT, n_tok)),
            dma((2 + CUT, n_tok)),
            dma((2 + CUT, n_tok)),
            dma((2 + CUT, n_tok)),
            dma((AG,)),
            dma((wide, AG)),
            dma((wide, AG)),
            dma((chips, AG)),
            dma((3, wide, CUT)),
            dma((3, wide, CUT)),
        ],
        compiler_params=pltpu.CompilerParams(
            collective_id=0, has_side_effects=True, vmem_limit_bytes=48 << 20
        ),
    )(
        *[
            pltpu.with_memory_space_constraint(operand, pltpu.HBM)
            for operand in (
                hidden_in[0], seg_ids, norm_gain1[None], jnp.transpose(rel_bias),
                norm_gain2[None], w_query, w_key_value, w_attn_out, w_in, w_out,
            )
        ]
    )
    return out[None]


def solution(mesh):
    placed = (
        P("blk", "tok", None),
        P("blk", None),
        P(),
        P(),
        P(),
        P(),
        P(),
        P(),
        P("blk", None),
        P("blk", None),
    )
    return jax.shard_map(
        functools.partial(per_device, mesh.shape["tok"], mesh.shape["blk"]),
        mesh=mesh, in_specs=placed, out_specs=P("blk", "tok", None), check_vma=False,
    )
```

```python
import functools

import jax
import jax.numpy as jnp
from jax import lax
from jax.experimental import pallas as pl
from jax.experimental.pallas import tpu as pltpu
from jax.sharding import PartitionSpec as P

D = 1024
HEADS = 16
HD = 64
BUCKETS = 32

bucket_bounds = (12, 16, 23, 32, 46, 64, 91)
epsilon = 1e-06
MESH = pl.DeviceIdType.MESH
VM = pl.BlockSpec(memory_space=pltpu.VMEM)
HBM = pl.BlockSpec(memory_space=pltpu.HBM)
CUT = 4
AG = 2
BY_Z = ()


def bucket_of(offset):
    distance = jnp.abs(offset)
    far_bucket = jnp.full_like(distance, 8)
    for boundary in bucket_bounds:
        far_bucket = far_bucket + (distance >= boundary).astype(jnp.int32)
    chosen = jnp.where(distance < 8, distance, far_bucket)
    return chosen + 16 * (offset > 0).astype(jnp.int32)


def rms_scale(values, gain):
    mean_square = jnp.mean(values * values, axis=-1, keepdims=True)
    return values * lax.rsqrt(mean_square + epsilon) * gain


def layer_kernel(
    WIDE,
    x_hbm, seg_hbm, g1_hbm, bias_hbm, g2_hbm, wq_hbm, wkv_hbm, wo_hbm, win_hbm, wout_hbm, out_ref,
    seg, g1, bias, g2, wq, wkv, wo, win, wout, hid, q_scr, kv_scr, att_scr, mid, gath, part,
    inbox, inner_scr,
    s_load, s_hid, r_hid, s_pair, r_pair, s_far, s_near, r_w, s_hand, r_hand, s_z, s_y, s_on, r_gath,
    s_out, r_in,
):
    tok = lax.axis_index("tok")
    blk = lax.axis_index("blk")
    c = lax.rem(blk, 2)
    chip = blk // 2
    y = lax.rem(chip, WIDE)
    z = chip // WIDE
    zp = z + 1 - 2 * lax.rem(z, 2)
    zq = 3 - z
    at_end = pl.when(lax.rem(z, 3) == 0)
    inside = pl.when(lax.rem(z, 3) != 0)
    oc = 1 - c
    n_tok, rows, _ = hid.shape
    units = win.shape[1]
    piece = units // n_tok
    cols = wout.shape[3]
    slots = 2 * WIDE
    n_in = 2 if piece % 32 == 0 else 1
    n_piece = n_in + CUT

    def dev(zz, yy, cc):
        return {"blk": (zz * WIDE + yy) * 2 + cc}

    def beside(d):
        return lax.rem(y + d, WIDE)

    def other_tok(d):
        return lax.rem(tok + d, n_tok)

    def remote(src, dst, ss, rs, to):
        return pltpu.make_async_remote_copy(
            src_ref=src, dst_ref=dst, send_sem=ss, recv_sem=rs, device_id=to, device_id_type=MESH
        )

    sides = range(1, WIDE)
    toks = range(1, n_tok)
    core_dev = dev(z, y, oc)
    near_dev = dev(zp, y, c)
    far_dev = dev(zq, y, c)

    barrier = pltpu.get_barrier_semaphore()
    greet = [core_dev, near_dev, far_dev]
    greet += [dev(z, beside(d), c) for d in sides] + [{"tok": other_tok(d)} for d in toks]
    for to in greet:
        pl.semaphore_signal(barrier, inc=1, device_id=to, device_id_type=MESH)

    wanted = [
        (x_hbm, hid.at[tok]), (g1_hbm, g1), (wq_hbm, wq), (seg_hbm, seg), (bias_hbm, bias),
        (wkv_hbm, wkv), (wo_hbm, wo), (g2_hbm, g2), (win_hbm, win.at[0]),
    ]
    wanted += [(wout_hbm.at[:, j * cols:(j + 1) * cols], wout.at[j, 0]) for j in range(CUT)]
    loads = [pltpu.make_async_copy(src, dst, s_load.at[k]) for k, (src, dst) in enumerate(wanted)]
    for load in loads:
        load.start()
    pl.semaphore_wait(barrier, len(greet))

    hid_copies = [
        remote(x_hbm, hid.at[tok], s_hid.at[d], r_hid.at[d], {"tok": other_tok(d)}) for d in toks
    ]
    for copy in hid_copies:
        copy.start()

    def ends(p, d):
        base = lax.rem(tok + n_tok - d, n_tok) * piece
        if p < n_in:
            size = piece // n_in
            spot = pl.ds(pl.multiple_of(base + p * size, size), size)
            return win_hbm.at[spot], win.at[2, spot], win.at[3, spot]
        spot = pl.ds(pl.multiple_of(base, piece), piece)
        j = p - n_in
        return wout.at[j, 0, spot], wout.at[j, 2, spot], wout.at[j, 3, spot]

    def far_copy(p):
        src, dst, _ = ends(p, 0)
        return remote(src, dst, s_far.at[p], r_w.at[p, 0], far_dev)

    def relay(p, d):
        spot = ends(p, 0)[1]
        return remote(spot, spot, s_near.at[p, d], r_w.at[p, d], {"tok": other_tok(d)})

    def hand_copy(p, d):
        _, src, dst = ends(p, d)
        return remote(src, dst, s_hand.at[p, d], r_hand.at[p, d], core_dev)

    def pair_copy(k):
        src, dst = (win_hbm, win.at[1]) if k == 0 else (wout.at[k - 1, 0], wout.at[k - 1, 1])
        return remote(src, dst, s_pair.at[k], r_pair.at[k], core_dev)

    def share(p):
        far_copy(p).wait_recv()
        for d in toks:
            relay(p, d).start()
        hand_copy(p, 0).start()

    def push(p, done):
        far_copy(done).wait_send()
        far_copy(p).start()

    def hand(p):
        for d in toks:
            relay(p, d).wait_recv()
            hand_copy(p, d).start()

    def have(p):
        for d in range(n_tok):
            hand_copy(p, d).wait_recv()

    for p in range(n_in):
        far_copy(p).start()
    pair_copy(0).start()

    loads[0].wait()
    loads[1].wait()
    normed = rms_scale(hid[tok].astype(jnp.float32), g1[...]).astype(jnp.bfloat16)
    loads[2].wait()
    q_scr[...] = jnp.dot(normed, wq[...], preferred_element_type=jnp.float32).astype(jnp.bfloat16)
    for load in loads[9:]:
        load.wait()
    for k in range(CUT):
        pair_copy(k + 1).start()
    loads[3].wait()
    loads[4].wait()
    loads[5].wait()

    def keys_values(values, who):
        kv_scr[pl.ds(pl.multiple_of(who * rows, rows), rows), :] = jnp.dot(
            values, wkv[...], preferred_element_type=jnp.float32
        ).astype(jnp.bfloat16)

    def seg_of(who):
        at = pl.ds(pl.multiple_of(who * rows, rows), rows)
        return jnp.broadcast_to(seg[:, at].astype(jnp.float32), (rows, rows))

    diagonal = lax.broadcasted_iota(jnp.int32, (rows, rows), 0) == (
        lax.broadcasted_iota(jnp.int32, (rows, rows), 1)
    )
    own_seg = jnp.sum(jnp.where(diagonal, seg_of(tok), 0.0), axis=-1, keepdims=True)
    low = lax.broadcasted_iota(jnp.int32, (rows, 2 * HD), 1) < HD
    zero = jnp.zeros((rows, 2 * HD), jnp.bfloat16)

    def both(values):
        return jnp.concatenate([jnp.where(low, values, zero), jnp.where(low, zero, values)], axis=0)

    def lines_of(who):
        spot = lax.broadcasted_iota(jnp.int32, (BUCKETS, 2 * rows), 1)
        offset = jnp.where(spot < rows, spot, spot - 2 * rows) + (who - tok) * rows
        chosen = lax.broadcasted_iota(jnp.int32, (BUCKETS, 2 * rows), 0) == bucket_of(offset)
        return jnp.dot(
            bias[...], chosen.astype(jnp.float32),
            precision=lax.Precision.HIGHEST, preferred_element_type=jnp.float32,
        )

    def attend(who, lines, same, state):
        held = pl.ds(pl.multiple_of(who * rows, rows), rows)
        found = []
        for pair in range(HEADS // 2):
            at = pair * 2 * HD
            scores = lax.dot_general(
                q_scr[:, at:at + 2 * HD], both(kv_scr[held, at:at + 2 * HD]),
                (((1,), (1,)), ((), ())), preferred_element_type=jnp.float32,
            )
            tops, totals, exps = [], [], []
            for half in range(2):
                head = 2 * pair + half
                line = jnp.broadcast_to(lines[head:head + 1, :], (rows, 2 * rows))
                shift = pltpu.roll(line, 0, 1, stride=1, stride_axis=0)[:, :rows]
                masked = jnp.where(same, scores[:, half * rows:(half + 1) * rows] + shift, -1e30)
                top = jnp.max(masked, axis=-1, keepdims=True)
                if state is not None:
                    top = jnp.maximum(top, state[pair][0][half])
                exp = jnp.exp(masked - top)
                tops.append(top)
                totals.append(jnp.sum(exp, axis=-1, keepdims=True))
                exps.append(exp.astype(jnp.bfloat16))
            mixed = jnp.dot(
                jnp.concatenate(exps, axis=1), both(kv_scr[held, D + at:D + at + 2 * HD]),
                preferred_element_type=jnp.float32,
            )
            if state is not None:
                old_tops, old_totals, old_mixed = state[pair]
                scale = [jnp.exp(old_tops[half] - tops[half]) for half in range(2)]
                totals = [totals[half] + scale[half] * old_totals[half] for half in range(2)]
                mixed = mixed + old_mixed * jnp.where(low, scale[0], scale[1])
            found.append((tops, totals, mixed))
        return found

    keys_values(normed, tok)
    state = attend(tok, lines_of(tok), own_seg == seg_of(tok), None)
    for d in toks:
        who = lax.rem(tok + n_tok - d, n_tok)
        lines = lines_of(who)
        same = own_seg == seg_of(who)
        if d == 1:
            @at_end
            def _():
                push(n_in, n_in - 1)

        hid_copies[d - 1].wait_recv()
        keys_values(rms_scale(hid[who].astype(jnp.float32), g1[...]).astype(jnp.bfloat16), who)
        if d == 1:
            for load in loads[6:9]:
                load.wait()
            @at_end
            def _():
                share(0)
                push(n_in + 1, n_in)

        state = attend(who, lines, same, state)
    for pair, (_, totals, mixed) in enumerate(state):
        at = pair * 2 * HD
        att_scr[:, at:at + 2 * HD] = (mixed / jnp.where(low, totals[0], totals[1])).astype(
            jnp.bfloat16
        )
    for p in range(1, n_in):
        at_end(functools.partial(share, p))
    middle = hid[tok].astype(jnp.float32) + jnp.dot(
        att_scr[...], wo[...], preferred_element_type=jnp.float32
    )
    mid[...] = middle
    gath[0] = rms_scale(middle, g2[...]).astype(jnp.bfloat16)

    ag_rows = rows // AG

    def rows_at(slot, h):
        return gath.at[slot, pl.ds(h * ag_rows, ag_rows)]

    def z_copy(h):
        return remote(rows_at(0, h), rows_at(WIDE, h), s_z.at[h], r_gath.at[WIDE, h], near_dev)

    def y_copy(d, h):
        slot = WIDE - d
        to = dev(z, beside(d), c)
        return remote(rows_at(0, h), rows_at(slot, h), s_y.at[d, h], r_gath.at[slot, h], to)

    def on_copy(d, h):
        if h in BY_Z:
            slot, to = WIDE + d, near_dev
            return remote(rows_at(d, h), rows_at(slot, h), s_on.at[d, h], r_gath.at[slot, h], to)
        slot, to = slots - d, dev(z, beside(d), c)
        return remote(rows_at(WIDE, h), rows_at(slot, h), s_on.at[d, h], r_gath.at[slot, h], to)

    def arrived(slot, h):
        remote(
            rows_at(slot, h), rows_at(slot, h), s_z.at[h], r_gath.at[slot, h], core_dev
        ).wait_recv()

    def first(lo, n, k, n_k):
        inner = lax.dot_general(
            gath[lo:lo + n].reshape(n * rows, D), win[k:k + n_k].reshape(n_k * units, D),
            (((1,), (1,)), ((), ())), preferred_element_type=jnp.float32,
        )
        inner_scr[lo * rows:(lo + n) * rows, k * units:(k + n_k) * units] = jnp.maximum(
            inner, 0.0
        ).astype(jnp.bfloat16)

    def second(j):
        terms = jnp.dot(
            inner_scr[...], wout[j].reshape(4 * units, cols), preferred_element_type=jnp.float32
        )
        at = slice(j * cols, (j + 1) * cols)
        mid[:, at] = mid[:, at] + terms[:rows]
        part[j] = terms.astype(jnp.bfloat16).reshape(slots, rows, cols)

    def send_sum(kind, d, slot, j, to):
        return remote(
            part.at[j, slot], inbox.at[kind, d, j], s_out.at[kind, d, j], r_in.at[kind, d, j], to
        )

    def corner_sum(d, j):
        to = dev(z, beside(d), c) if j % 2 == 0 else near_dev
        return send_sum(0, d, WIDE + d, j, to)

    def side_sum(d, j):
        return send_sum(1, d, d, j, dev(z, beside(d), c))

    def near_sum(j):
        return send_sum(2, 0, WIDE, j, near_dev)

    def got(kind, d, j):
        send_sum(kind, d, 0, j, core_dev).wait_recv()
        return inbox[kind, d, j].astype(jnp.float32)

    def send(j):
        for d in sides:
            corner_sum(d, j).start()
        if j % 2 == 0:
            for d in sides:
                side_sum(d, j).start()
        else:
            near_sum(j).start()

    def merge(j):
        if j % 2 == 0:
            extra = got(0, 1, j)
            for d in sides[1:]:
                extra = extra + got(0, d, j)
            part[j, WIDE] = (part[j, WIDE].astype(jnp.float32) + extra).astype(jnp.bfloat16)
            near_sum(j).start()
        else:
            for d in sides:
                part[j, d] = (part[j, d].astype(jnp.float32) + got(0, d, j)).astype(jnp.bfloat16)
                side_sum(d, j).start()

    for h in range(AG):
        z_copy(h).start()
        for d in sides:
            y_copy(d, h).start()
    w0, w1, w2, w3 = range(n_in, n_piece)

    @inside
    def _():
        push(w0, n_in - 1)
        far_copy(w1).start()

    pair_copy(0).wait_recv()
    first(0, 1, 0, 2)
    at_end(lambda: share(w0))

    def pass_on(h):
        if h in BY_Z:
            for d in sides:
                arrived(d, h)
                on_copy(d, h).start()
        else:
            arrived(WIDE, h)
            for d in sides:
                on_copy(d, h).start()

    for h in range(AG // 2):
        pass_on(h)

    @inside
    def _():
        for p in range(n_in):
            share(p)

    for h in range(AG // 2, AG):
        pass_on(h)

    @inside
    def _():
        push(w2, w0)
        push(w3, w1)
        share(w0)
        share(w1)

    @at_end
    def _():
        share(w1)
        push(w2, w1)
        far_copy(w3).start()

    for p in range(n_in):
        hand(p)
    for h in range(AG):
        if h in BY_Z:
            arrived(WIDE, h)
        else:
            for d in sides:
                arrived(d, h)
    first(1, WIDE, 0, 2)

    @inside
    def _():
        share(w2)
        share(w3)

    for p in range(n_in):
        have(p)
    first(0, WIDE + 1, 2, 2)

    hand(w0)
    for d in sides:
        for h in range(AG):
            arrived(WIDE + d, h)
    first(WIDE + 1, WIDE - 1, 0, 4)
    for k in range(CUT):
        pair_copy(k + 1).wait_recv()
    hand(w1)
    have(w0)
    second(0)
    send(0)

    @at_end
    def _():
        share(w2)
        share(w3)

    have(w1)
    second(1)
    send(1)
    hand(w2)
    merge(0)
    hand(w3)
    have(w2)
    second(2)
    send(2)
    merge(1)
    have(w3)
    second(3)
    send(3)
    merge(2)
    merge(3)
    for j in range(CUT):
        at = slice(j * cols, (j + 1) * cols)
        total = mid[:, at]
        for d in sides:
            total = total + got(1, d, j)
        total = total + got(2, 0, j)
        out_ref[:, at] = total.astype(jnp.bfloat16)

    for copy in hid_copies:
        copy.wait_send()
    for k in range(1 + CUT):
        pair_copy(k).wait_send()
    for p in (*range(n_in - 1), w2, w3):
        far_copy(p).wait_send()
    for p in range(n_piece):
        for d in toks:
            relay(p, d).wait_send()
        for d in range(n_tok):
            hand_copy(p, d).wait_send()
    for h in range(AG):
        z_copy(h).wait_send()
        for d in sides:
            y_copy(d, h).wait_send()
            on_copy(d, h).wait_send()
    for j in range(CUT):
        for d in sides:
            corner_sum(d, j).wait_send()
            side_sum(d, j).wait_send()
        near_sum(j).wait_send()


def per_device(
    n_tok, n_blk, hidden_in, seg_ids, norm_gain1, w_query, w_key_value, rel_bias, w_attn_out,
    norm_gain2, w_in, w_out,
):
    rows = hidden_in.shape[1]
    count = n_tok * rows
    units = w_in.shape[0]
    wide = n_blk // 8
    chips = 2 * wide
    cols = D // CUT
    dma = pltpu.SemaphoreType.DMA

    def half(*shape):
        return pltpu.VMEM(shape, jnp.bfloat16)

    def full(*shape):
        return pltpu.VMEM(shape, jnp.float32)

    out = pl.pallas_call(
        functools.partial(layer_kernel, wide),
        out_shape=jax.ShapeDtypeStruct((rows, D), jnp.bfloat16),
        in_specs=[HBM] * 10,
        out_specs=VM,
        scratch_shapes=[
            pltpu.VMEM((1, count), jnp.int32),
            full(1, D),
            full(HEADS, BUCKETS),
            full(1, D),
            half(D, D),
            half(D, 2 * D),
            half(D, D),
            half(4, units, D),
            half(CUT, 4, units, cols),
            half(n_tok, rows, D),
            half(rows, D),
            half(count, 2 * D),
            half(rows, D),
            full(rows, D),
            half(chips, rows, D),
            half(CUT, chips, rows, cols),
            half(3, wide, CUT, rows, cols),
            half(chips * rows, 4 * units),
            dma((9 + CUT,)),
            dma((n_tok,)),
            dma((n_tok,)),
            dma((1 + CUT,)),
            dma((1 + CUT,)),
            dma((2 + CUT,)),
            dma((2 + CUT, n_tok)),
            dma((2 + CUT, n_tok)),
            dma((2 + CUT, n_tok)),
            dma((2 + CUT, n_tok)),
            dma((AG,)),
            dma((wide, AG)),
            dma((wide, AG)),
            dma((chips, AG)),
            dma((3, wide, CUT)),
            dma((3, wide, CUT)),
        ],
        compiler_params=pltpu.CompilerParams(
            collective_id=0, has_side_effects=True, vmem_limit_bytes=48 << 20
        ),
    )(
        *[
            pltpu.with_memory_space_constraint(operand, pltpu.HBM)
            for operand in (
                hidden_in[0], seg_ids, norm_gain1[None], jnp.transpose(rel_bias),
                norm_gain2[None], w_query, w_key_value, w_attn_out, w_in, w_out,
            )
        ]
    )
    return out[None]


def solution(mesh):
    placed = (
        P("blk", "tok", None),
        P("blk", None),
        P(),
        P(),
        P(),
        P(),
        P(),
        P(),
        P("blk", None),
        P("blk", None),
    )
    return jax.shard_map(
        functools.partial(per_device, mesh.shape["tok"], mesh.shape["blk"]),
        mesh=mesh, in_specs=placed, out_specs=P("blk", "tok", None), check_vma=False,
    )
```

```python
import functools

import jax
import jax.numpy as jnp
from jax import lax
from jax.experimental import pallas as pl
from jax.experimental.pallas import tpu as pltpu
from jax.sharding import PartitionSpec as P

D = 1024
HEADS = 16
HD = 64
BUCKETS = 32

bucket_bounds = (12, 16, 23, 32, 46, 64, 91)
epsilon = 1e-06
MESH = pl.DeviceIdType.MESH
VM = pl.BlockSpec(memory_space=pltpu.VMEM)
HBM = pl.BlockSpec(memory_space=pltpu.HBM)
CUT = 4
AG = 2
BY_Z = ()


def bucket_of(offset):
    distance = jnp.abs(offset)
    far_bucket = jnp.full_like(distance, 8)
    for boundary in bucket_bounds:
        far_bucket = far_bucket + (distance >= boundary).astype(jnp.int32)
    chosen = jnp.where(distance < 8, distance, far_bucket)
    return chosen + 16 * (offset > 0).astype(jnp.int32)


def rms_scale(values, gain):
    mean_square = jnp.mean(values * values, axis=-1, keepdims=True)
    return values * lax.rsqrt(mean_square + epsilon) * gain


def layer_kernel(
    WIDE,
    x_hbm, seg_hbm, g1_hbm, bias_hbm, g2_hbm, wq_hbm, wkv_hbm, wo_hbm, win_hbm, wout_hbm, out_ref,
    seg, g1, bias, g2, wq, wkv, wo, win, wout, hid, q_scr, kv_scr, att_scr, mid, gath, part,
    inbox, inner_scr,
    s_load, s_hid, r_hid, s_pair, r_pair, s_far, s_near, r_w, s_hand, r_hand, s_z, s_y, s_on, r_gath,
    s_out, r_in,
):
    tok = lax.axis_index("tok")
    blk = lax.axis_index("blk")
    c = lax.rem(blk, 2)
    chip = blk // 2
    y = lax.rem(chip, WIDE)
    z = chip // WIDE
    zp = z + 1 - 2 * lax.rem(z, 2)
    zq = 3 - z
    at_end = pl.when(lax.rem(z, 3) == 0)
    inside = pl.when(lax.rem(z, 3) != 0)
    oc = 1 - c
    n_tok, rows, _ = hid.shape
    units = win.shape[1]
    piece = units // n_tok
    cols = wout.shape[3]
    slots = 2 * WIDE
    n_in = 2 if piece % 32 == 0 else 1
    n_piece = n_in + CUT

    def dev(zz, yy, cc):
        return {"blk": (zz * WIDE + yy) * 2 + cc}

    def beside(d):
        return lax.rem(y + d, WIDE)

    def other_tok(d):
        return lax.rem(tok + d, n_tok)

    def remote(src, dst, ss, rs, to):
        return pltpu.make_async_remote_copy(
            src_ref=src, dst_ref=dst, send_sem=ss, recv_sem=rs, device_id=to, device_id_type=MESH
        )

    sides = range(1, WIDE)
    toks = range(1, n_tok)
    core_dev = dev(z, y, oc)
    near_dev = dev(zp, y, c)
    far_dev = dev(zq, y, c)

    barrier = pltpu.get_barrier_semaphore()
    greet = [core_dev, near_dev, far_dev]
    greet += [dev(z, beside(d), c) for d in sides] + [{"tok": other_tok(d)} for d in toks]
    for to in greet:
        pl.semaphore_signal(barrier, inc=1, device_id=to, device_id_type=MESH)

    wanted = [
        (x_hbm, hid.at[tok]), (g1_hbm, g1), (wq_hbm, wq), (seg_hbm, seg), (bias_hbm, bias),
        (wkv_hbm, wkv), (wo_hbm, wo), (g2_hbm, g2), (win_hbm, win.at[0]),
    ]
    wanted += [(wout_hbm.at[:, j * cols:(j + 1) * cols], wout.at[j, 0]) for j in range(CUT)]
    loads = [pltpu.make_async_copy(src, dst, s_load.at[k]) for k, (src, dst) in enumerate(wanted)]
    for load in loads:
        load.start()
    pl.semaphore_wait(barrier, len(greet))

    hid_copies = [
        remote(x_hbm, hid.at[tok], s_hid.at[d], r_hid.at[d], {"tok": other_tok(d)}) for d in toks
    ]
    for copy in hid_copies:
        copy.start()

    def ends(p, d):
        base = lax.rem(tok + n_tok - d, n_tok) * piece
        if p < n_in:
            size = piece // n_in
            spot = pl.ds(pl.multiple_of(base + p * size, size), size)
            return win_hbm.at[spot], win.at[2, spot], win.at[3, spot]
        spot = pl.ds(pl.multiple_of(base, piece), piece)
        j = p - n_in
        return wout.at[j, 0, spot], wout.at[j, 2, spot], wout.at[j, 3, spot]

    def far_copy(p):
        src, dst, _ = ends(p, 0)
        return remote(src, dst, s_far.at[p], r_w.at[p, 0], far_dev)

    def relay(p, d):
        spot = ends(p, 0)[1]
        return remote(spot, spot, s_near.at[p, d], r_w.at[p, d], {"tok": other_tok(d)})

    def hand_copy(p, d):
        _, src, dst = ends(p, d)
        return remote(src, dst, s_hand.at[p, d], r_hand.at[p, d], core_dev)

    def pair_copy(k):
        src, dst = (win_hbm, win.at[1]) if k == 0 else (wout.at[k - 1, 0], wout.at[k - 1, 1])
        return remote(src, dst, s_pair.at[k], r_pair.at[k], core_dev)

    def share(p):
        far_copy(p).wait_recv()
        for d in toks:
            relay(p, d).start()
        hand_copy(p, 0).start()

    def push(p, done):
        far_copy(done).wait_send()
        far_copy(p).start()

    def hand(p):
        for d in toks:
            relay(p, d).wait_recv()
            hand_copy(p, d).start()

    def have(p):
        for d in range(n_tok):
            hand_copy(p, d).wait_recv()

    for p in range(n_in):
        far_copy(p).start()
    pair_copy(0).start()

    loads[0].wait()
    loads[1].wait()
    normed = rms_scale(hid[tok].astype(jnp.float32), g1[...]).astype(jnp.bfloat16)
    loads[2].wait()
    q_scr[...] = jnp.dot(normed, wq[...], preferred_element_type=jnp.float32).astype(jnp.bfloat16)
    for load in loads[9:]:
        load.wait()
    for k in range(CUT):
        pair_copy(k + 1).start()
    loads[3].wait()
    loads[4].wait()
    loads[5].wait()

    def keys_values(values, who):
        kv_scr[pl.ds(pl.multiple_of(who * rows, rows), rows), :] = jnp.dot(
            values, wkv[...], preferred_element_type=jnp.float32
        ).astype(jnp.bfloat16)

    def seg_of(who):
        at = pl.ds(pl.multiple_of(who * rows, rows), rows)
        return jnp.broadcast_to(seg[:, at].astype(jnp.float32), (rows, rows))

    diagonal = lax.broadcasted_iota(jnp.int32, (rows, rows), 0) == (
        lax.broadcasted_iota(jnp.int32, (rows, rows), 1)
    )
    own_seg = jnp.sum(jnp.where(diagonal, seg_of(tok), 0.0), axis=-1, keepdims=True)
    low = lax.broadcasted_iota(jnp.int32, (rows, 2 * HD), 1) < HD
    zero = jnp.zeros((rows, 2 * HD), jnp.bfloat16)

    def both(values):
        return jnp.concatenate([jnp.where(low, values, zero), jnp.where(low, zero, values)], axis=0)

    def lines_of(who):
        spot = lax.broadcasted_iota(jnp.int32, (BUCKETS, 2 * rows), 1)
        offset = jnp.where(spot < rows, spot, spot - 2 * rows) + (who - tok) * rows
        chosen = lax.broadcasted_iota(jnp.int32, (BUCKETS, 2 * rows), 0) == bucket_of(offset)
        return jnp.dot(
            bias[...], chosen.astype(jnp.float32),
            precision=lax.Precision.HIGHEST, preferred_element_type=jnp.float32,
        )

    def attend(who, lines, same, state):
        held = pl.ds(pl.multiple_of(who * rows, rows), rows)
        found = []
        for pair in range(HEADS // 2):
            at = pair * 2 * HD
            scores = lax.dot_general(
                q_scr[:, at:at + 2 * HD], both(kv_scr[held, at:at + 2 * HD]),
                (((1,), (1,)), ((), ())), preferred_element_type=jnp.float32,
            )
            tops, totals, exps = [], [], []
            for half in range(2):
                head = 2 * pair + half
                line = jnp.broadcast_to(lines[head:head + 1, :], (rows, 2 * rows))
                shift = pltpu.roll(line, 0, 1, stride=1, stride_axis=0)[:, :rows]
                masked = jnp.where(same, scores[:, half * rows:(half + 1) * rows] + shift, -1e30)
                top = jnp.max(masked, axis=-1, keepdims=True)
                if state is not None:
                    top = jnp.maximum(top, state[pair][0][half])
                exp = jnp.exp(masked - top)
                tops.append(top)
                totals.append(jnp.sum(exp, axis=-1, keepdims=True))
                exps.append(exp.astype(jnp.bfloat16))
            mixed = jnp.dot(
                jnp.concatenate(exps, axis=1), both(kv_scr[held, D + at:D + at + 2 * HD]),
                preferred_element_type=jnp.float32,
            )
            if state is not None:
                old_tops, old_totals, old_mixed = state[pair]
                scale = [jnp.exp(old_tops[half] - tops[half]) for half in range(2)]
                totals = [totals[half] + scale[half] * old_totals[half] for half in range(2)]
                mixed = mixed + old_mixed * jnp.where(low, scale[0], scale[1])
            found.append((tops, totals, mixed))
        return found

    keys_values(normed, tok)
    state = attend(tok, lines_of(tok), own_seg == seg_of(tok), None)
    for d in toks:
        who = lax.rem(tok + n_tok - d, n_tok)
        lines = lines_of(who)
        same = own_seg == seg_of(who)
        if d == 1:
            @at_end
            def _():
                push(n_in, n_in - 1)

        hid_copies[d - 1].wait_recv()
        keys_values(rms_scale(hid[who].astype(jnp.float32), g1[...]).astype(jnp.bfloat16), who)
        if d == 1:
            for load in loads[6:9]:
                load.wait()
            @at_end
            def _():
                share(0)
                push(n_in + 1, n_in)

        state = attend(who, lines, same, state)
    for pair, (_, totals, mixed) in enumerate(state):
        at = pair * 2 * HD
        att_scr[:, at:at + 2 * HD] = (mixed / jnp.where(low, totals[0], totals[1])).astype(
            jnp.bfloat16
        )
    for p in range(1, n_in):
        at_end(functools.partial(share, p))
    middle = hid[tok].astype(jnp.float32) + jnp.dot(
        att_scr[...], wo[...], preferred_element_type=jnp.float32
    )
    mid[...] = middle
    gath[0] = rms_scale(middle, g2[...]).astype(jnp.bfloat16)

    ag_rows = rows // AG

    def rows_at(slot, h):
        return gath.at[slot, pl.ds(h * ag_rows, ag_rows)]

    def z_copy(h):
        return remote(rows_at(0, h), rows_at(WIDE, h), s_z.at[h], r_gath.at[WIDE, h], near_dev)

    def y_copy(d, h):
        slot = WIDE - d
        to = dev(z, beside(d), c)
        return remote(rows_at(0, h), rows_at(slot, h), s_y.at[d, h], r_gath.at[slot, h], to)

    def on_copy(d, h):
        if h in BY_Z:
            slot, to = WIDE + d, near_dev
            return remote(rows_at(d, h), rows_at(slot, h), s_on.at[d, h], r_gath.at[slot, h], to)
        slot, to = slots - d, dev(z, beside(d), c)
        return remote(rows_at(WIDE, h), rows_at(slot, h), s_on.at[d, h], r_gath.at[slot, h], to)

    def arrived(slot, h):
        remote(
            rows_at(slot, h), rows_at(slot, h), s_z.at[h], r_gath.at[slot, h], core_dev
        ).wait_recv()

    def first(lo, n, k, n_k):
        inner = lax.dot_general(
            gath[lo:lo + n].reshape(n * rows, D), win[k:k + n_k].reshape(n_k * units, D),
            (((1,), (1,)), ((), ())), preferred_element_type=jnp.float32,
        )
        inner_scr[lo * rows:(lo + n) * rows, k * units:(k + n_k) * units] = jnp.maximum(
            inner, 0.0
        ).astype(jnp.bfloat16)

    def second(j):
        terms = jnp.dot(
            inner_scr[...], wout[j].reshape(4 * units, cols), preferred_element_type=jnp.float32
        )
        at = slice(j * cols, (j + 1) * cols)
        mid[:, at] = mid[:, at] + terms[:rows]
        part[j] = terms.astype(jnp.bfloat16).reshape(slots, rows, cols)

    def send_sum(kind, d, slot, j, to):
        return remote(
            part.at[j, slot], inbox.at[kind, d, j], s_out.at[kind, d, j], r_in.at[kind, d, j], to
        )

    def corner_sum(d, j):
        to = dev(z, beside(d), c) if j % 2 == 0 else near_dev
        return send_sum(0, d, WIDE + d, j, to)

    def side_sum(d, j):
        return send_sum(1, d, d, j, dev(z, beside(d), c))

    def near_sum(j):
        return send_sum(2, 0, WIDE, j, near_dev)

    def got(kind, d, j):
        send_sum(kind, d, 0, j, core_dev).wait_recv()
        return inbox[kind, d, j].astype(jnp.float32)

    def send(j):
        for d in sides:
            corner_sum(d, j).start()
        if j % 2 == 0:
            for d in sides:
                side_sum(d, j).start()
        else:
            near_sum(j).start()

    def merge(j):
        if j % 2 == 0:
            extra = got(0, 1, j)
            for d in sides[1:]:
                extra = extra + got(0, d, j)
            part[j, WIDE] = (part[j, WIDE].astype(jnp.float32) + extra).astype(jnp.bfloat16)
            near_sum(j).start()
        else:
            for d in sides:
                part[j, d] = (part[j, d].astype(jnp.float32) + got(0, d, j)).astype(jnp.bfloat16)
                side_sum(d, j).start()

    for h in range(AG):
        z_copy(h).start()
        for d in sides:
            y_copy(d, h).start()
    w0, w1, w2, w3 = range(n_in, n_piece)

    pair_copy(0).wait_recv()
    first(0, 1, 0, 2)
    @inside
    def _():
        push(w0, n_in - 1)
        far_copy(w1).start()
        for p in range(n_in):
            share(p)

    at_end(lambda: share(w0))

    def pass_on(h):
        if h in BY_Z:
            for d in sides:
                arrived(d, h)
                on_copy(d, h).start()
        else:
            arrived(WIDE, h)
            for d in sides:
                on_copy(d, h).start()

    for h in range(AG // 2):
        pass_on(h)

    @at_end
    def _():
        for p in range(n_in):
            hand(p)

    for h in range(AG // 2, AG):
        pass_on(h)

    @inside
    def _():
        push(w2, w0)
        push(w3, w1)
        share(w0)
        share(w1)

    @at_end
    def _():
        share(w1)
        push(w2, w1)
        far_copy(w3).start()

    @inside
    def _():
        for p in range(n_in):
            hand(p)

    for h in range(AG):
        if h in BY_Z:
            arrived(WIDE, h)
        else:
            for d in sides:
                arrived(d, h)
    first(1, WIDE, 0, 2)

    @inside
    def _():
        share(w2)
        share(w3)

    for p in range(n_in):
        have(p)
    first(0, WIDE + 1, 2, 2)

    hand(w0)
    for d in sides:
        for h in range(AG):
            arrived(WIDE + d, h)
    first(WIDE + 1, WIDE - 1, 0, 4)
    for k in range(CUT):
        pair_copy(k + 1).wait_recv()
    hand(w1)
    have(w0)
    second(0)
    send(0)

    @at_end
    def _():
        share(w2)
        share(w3)

    have(w1)
    second(1)
    send(1)
    hand(w2)
    merge(0)
    hand(w3)
    have(w2)
    second(2)
    send(2)
    merge(1)
    have(w3)
    second(3)
    send(3)
    merge(2)
    merge(3)
    for j in range(CUT):
        at = slice(j * cols, (j + 1) * cols)
        total = mid[:, at]
        for d in sides:
            total = total + got(1, d, j)
        total = total + got(2, 0, j)
        out_ref[:, at] = total.astype(jnp.bfloat16)

    for copy in hid_copies:
        copy.wait_send()
    for k in range(1 + CUT):
        pair_copy(k).wait_send()
    for p in (*range(n_in - 1), w2, w3):
        far_copy(p).wait_send()
    for p in range(n_piece):
        for d in toks:
            relay(p, d).wait_send()
        for d in range(n_tok):
            hand_copy(p, d).wait_send()
    for h in range(AG):
        z_copy(h).wait_send()
        for d in sides:
            y_copy(d, h).wait_send()
            on_copy(d, h).wait_send()
    for j in range(CUT):
        for d in sides:
            corner_sum(d, j).wait_send()
            side_sum(d, j).wait_send()
        near_sum(j).wait_send()


def per_device(
    n_tok, n_blk, hidden_in, seg_ids, norm_gain1, w_query, w_key_value, rel_bias, w_attn_out,
    norm_gain2, w_in, w_out,
):
    rows = hidden_in.shape[1]
    count = n_tok * rows
    units = w_in.shape[0]
    wide = n_blk // 8
    chips = 2 * wide
    cols = D // CUT
    dma = pltpu.SemaphoreType.DMA

    def half(*shape):
        return pltpu.VMEM(shape, jnp.bfloat16)

    def full(*shape):
        return pltpu.VMEM(shape, jnp.float32)

    out = pl.pallas_call(
        functools.partial(layer_kernel, wide),
        out_shape=jax.ShapeDtypeStruct((rows, D), jnp.bfloat16),
        in_specs=[HBM] * 10,
        out_specs=VM,
        scratch_shapes=[
            pltpu.VMEM((1, count), jnp.int32),
            full(1, D),
            full(HEADS, BUCKETS),
            full(1, D),
            half(D, D),
            half(D, 2 * D),
            half(D, D),
            half(4, units, D),
            half(CUT, 4, units, cols),
            half(n_tok, rows, D),
            half(rows, D),
            half(count, 2 * D),
            half(rows, D),
            full(rows, D),
            half(chips, rows, D),
            half(CUT, chips, rows, cols),
            half(3, wide, CUT, rows, cols),
            half(chips * rows, 4 * units),
            dma((9 + CUT,)),
            dma((n_tok,)),
            dma((n_tok,)),
            dma((1 + CUT,)),
            dma((1 + CUT,)),
            dma((2 + CUT,)),
            dma((2 + CUT, n_tok)),
            dma((2 + CUT, n_tok)),
            dma((2 + CUT, n_tok)),
            dma((2 + CUT, n_tok)),
            dma((AG,)),
            dma((wide, AG)),
            dma((wide, AG)),
            dma((chips, AG)),
            dma((3, wide, CUT)),
            dma((3, wide, CUT)),
        ],
        compiler_params=pltpu.CompilerParams(
            collective_id=0, has_side_effects=True, vmem_limit_bytes=48 << 20
        ),
    )(
        *[
            pltpu.with_memory_space_constraint(operand, pltpu.HBM)
            for operand in (
                hidden_in[0], seg_ids, norm_gain1[None], jnp.transpose(rel_bias),
                norm_gain2[None], w_query, w_key_value, w_attn_out, w_in, w_out,
            )
        ]
    )
    return out[None]


def solution(mesh):
    placed = (
        P("blk", "tok", None),
        P("blk", None),
        P(),
        P(),
        P(),
        P(),
        P(),
        P(),
        P("blk", None),
        P("blk", None),
    )
    return jax.shard_map(
        functools.partial(per_device, mesh.shape["tok"], mesh.shape["blk"]),
        mesh=mesh, in_specs=placed, out_specs=P("blk", "tok", None), check_vma=False,
    )
```

```python
import functools

import jax
import jax.numpy as jnp
from jax import lax
from jax.experimental import pallas as pl
from jax.experimental.pallas import tpu as pltpu
from jax.sharding import PartitionSpec as P

D = 1024
HEADS = 16
HD = 64
BUCKETS = 32

bucket_bounds = (12, 16, 23, 32, 46, 64, 91)
epsilon = 1e-06
MESH = pl.DeviceIdType.MESH
VM = pl.BlockSpec(memory_space=pltpu.VMEM)
HBM = pl.BlockSpec(memory_space=pltpu.HBM)
CUT = 4
AG = 2
BY_Z = ()


def bucket_of(offset):
    distance = jnp.abs(offset)
    far_bucket = jnp.full_like(distance, 8)
    for boundary in bucket_bounds:
        far_bucket = far_bucket + (distance >= boundary).astype(jnp.int32)
    chosen = jnp.where(distance < 8, distance, far_bucket)
    return chosen + 16 * (offset > 0).astype(jnp.int32)


def rms_scale(values, gain):
    mean_square = jnp.mean(values * values, axis=-1, keepdims=True)
    return values * lax.rsqrt(mean_square + epsilon) * gain


def layer_kernel(
    WIDE,
    x_hbm, seg_hbm, g1_hbm, bias_hbm, g2_hbm, wq_hbm, wkv_hbm, wo_hbm, win_hbm, wout_hbm, out_ref,
    seg, g1, bias, g2, wq, wkv, wo, win, wout, hid, q_scr, kv_scr, att_scr, mid, gath, part,
    inbox, inner_scr,
    s_load, s_hid, r_hid, s_pair, r_pair, s_far, s_near, r_w, s_hand, r_hand, s_z, s_y, s_on, r_gath,
    s_out, r_in,
):
    tok = lax.axis_index("tok")
    blk = lax.axis_index("blk")
    c = lax.rem(blk, 2)
    chip = blk // 2
    y = lax.rem(chip, WIDE)
    z = chip // WIDE
    zp = z + 1 - 2 * lax.rem(z, 2)
    zq = 3 - z
    at_end = pl.when(lax.rem(z, 3) == 0)
    inside = pl.when(lax.rem(z, 3) != 0)
    oc = 1 - c
    n_tok, rows, _ = hid.shape
    units = win.shape[1]
    piece = units // n_tok
    cols = wout.shape[3]
    slots = 2 * WIDE
    n_in = 2 if piece % 32 == 0 else 1
    n_piece = n_in + CUT

    def dev(zz, yy, cc):
        return {"blk": (zz * WIDE + yy) * 2 + cc}

    def beside(d):
        return lax.rem(y + d, WIDE)

    def other_tok(d):
        return lax.rem(tok + d, n_tok)

    def remote(src, dst, ss, rs, to):
        return pltpu.make_async_remote_copy(
            src_ref=src, dst_ref=dst, send_sem=ss, recv_sem=rs, device_id=to, device_id_type=MESH
        )

    sides = range(1, WIDE)
    toks = range(1, n_tok)
    core_dev = dev(z, y, oc)
    near_dev = dev(zp, y, c)
    far_dev = dev(zq, y, c)

    barrier = pltpu.get_barrier_semaphore()
    greet = [core_dev, near_dev, far_dev]
    greet += [dev(z, beside(d), c) for d in sides] + [{"tok": other_tok(d)} for d in toks]
    for to in greet:
        pl.semaphore_signal(barrier, inc=1, device_id=to, device_id_type=MESH)

    wanted = [
        (x_hbm, hid.at[tok]), (g1_hbm, g1), (wq_hbm, wq), (seg_hbm, seg), (bias_hbm, bias),
        (wkv_hbm, wkv), (wo_hbm, wo), (g2_hbm, g2), (win_hbm, win.at[0]),
    ]
    wanted += [(wout_hbm.at[:, j * cols:(j + 1) * cols], wout.at[j, 0]) for j in range(CUT)]
    loads = [pltpu.make_async_copy(src, dst, s_load.at[k]) for k, (src, dst) in enumerate(wanted)]
    for load in loads:
        load.start()
    pl.semaphore_wait(barrier, len(greet))

    hid_copies = [
        remote(x_hbm, hid.at[tok], s_hid.at[d], r_hid.at[d], {"tok": other_tok(d)}) for d in toks
    ]
    for copy in hid_copies:
        copy.start()

    def ends(p, d):
        base = lax.rem(tok + n_tok - d, n_tok) * piece
        if p < n_in:
            size = piece // n_in
            spot = pl.ds(pl.multiple_of(base + p * size, size), size)
            return win_hbm.at[spot], win.at[2, spot], win.at[3, spot]
        spot = pl.ds(pl.multiple_of(base, piece), piece)
        j = p - n_in
        return wout.at[j, 0, spot], wout.at[j, 2, spot], wout.at[j, 3, spot]

    def far_copy(p):
        src, dst, _ = ends(p, 0)
        return remote(src, dst, s_far.at[p], r_w.at[p, 0], far_dev)

    def relay(p, d):
        spot = ends(p, 0)[1]
        return remote(spot, spot, s_near.at[p, d], r_w.at[p, d], {"tok": other_tok(d)})

    def hand_copy(p, d):
        _, src, dst = ends(p, d)
        return remote(src, dst, s_hand.at[p, d], r_hand.at[p, d], core_dev)

    def pair_copy(k):
        src, dst = (win_hbm, win.at[1]) if k == 0 else (wout.at[k - 1, 0], wout.at[k - 1, 1])
        return remote(src, dst, s_pair.at[k], r_pair.at[k], core_dev)

    def share(p):
        far_copy(p).wait_recv()
        for d in toks:
            relay(p, d).start()
        hand_copy(p, 0).start()

    def push(p, done):
        far_copy(done).wait_send()
        far_copy(p).start()

    def hand(p):
        for d in toks:
            relay(p, d).wait_recv()
            hand_copy(p, d).start()

    def have(p):
        for d in range(n_tok):
            hand_copy(p, d).wait_recv()

    for p in range(n_in):
        far_copy(p).start()
    pair_copy(0).start()

    loads[0].wait()
    loads[1].wait()
    normed = rms_scale(hid[tok].astype(jnp.float32), g1[...]).astype(jnp.bfloat16)
    loads[2].wait()
    q_scr[...] = jnp.dot(normed, wq[...], preferred_element_type=jnp.float32).astype(jnp.bfloat16)
    for load in loads[9:]:
        load.wait()
    for k in range(CUT):
        pair_copy(k + 1).start()
    loads[3].wait()
    loads[4].wait()
    loads[5].wait()

    def keys_values(values, who):
        kv_scr[pl.ds(pl.multiple_of(who * rows, rows), rows), :] = jnp.dot(
            values, wkv[...], preferred_element_type=jnp.float32
        ).astype(jnp.bfloat16)

    def seg_of(who):
        at = pl.ds(pl.multiple_of(who * rows, rows), rows)
        return jnp.broadcast_to(seg[:, at].astype(jnp.float32), (rows, rows))

    diagonal = lax.broadcasted_iota(jnp.int32, (rows, rows), 0) == (
        lax.broadcasted_iota(jnp.int32, (rows, rows), 1)
    )
    own_seg = jnp.sum(jnp.where(diagonal, seg_of(tok), 0.0), axis=-1, keepdims=True)
    low = lax.broadcasted_iota(jnp.int32, (rows, 2 * HD), 1) < HD
    zero = jnp.zeros((rows, 2 * HD), jnp.bfloat16)

    def both(values):
        return jnp.concatenate([jnp.where(low, values, zero), jnp.where(low, zero, values)], axis=0)

    def lines_of(who):
        spot = lax.broadcasted_iota(jnp.int32, (BUCKETS, 2 * rows), 1)
        offset = jnp.where(spot < rows, spot, spot - 2 * rows) + (who - tok) * rows
        chosen = lax.broadcasted_iota(jnp.int32, (BUCKETS, 2 * rows), 0) == bucket_of(offset)
        return jnp.dot(
            bias[...], chosen.astype(jnp.float32),
            precision=lax.Precision.HIGHEST, preferred_element_type=jnp.float32,
        )

    def attend(who, lines, same, state):
        held = pl.ds(pl.multiple_of(who * rows, rows), rows)
        found = []
        for pair in range(HEADS // 2):
            at = pair * 2 * HD
            scores = lax.dot_general(
                q_scr[:, at:at + 2 * HD], both(kv_scr[held, at:at + 2 * HD]),
                (((1,), (1,)), ((), ())), preferred_element_type=jnp.float32,
            )
            tops, totals, exps = [], [], []
            for half in range(2):
                head = 2 * pair + half
                line = jnp.broadcast_to(lines[head:head + 1, :], (rows, 2 * rows))
                shift = pltpu.roll(line, 0, 1, stride=1, stride_axis=0)[:, :rows]
                masked = jnp.where(same, scores[:, half * rows:(half + 1) * rows] + shift, -1e30)
                top = jnp.max(masked, axis=-1, keepdims=True)
                if state is not None:
                    top = jnp.maximum(top, state[pair][0][half])
                exp = jnp.exp(masked - top)
                tops.append(top)
                totals.append(jnp.sum(exp, axis=-1, keepdims=True))
                exps.append(exp.astype(jnp.bfloat16))
            mixed = jnp.dot(
                jnp.concatenate(exps, axis=1), both(kv_scr[held, D + at:D + at + 2 * HD]),
                preferred_element_type=jnp.float32,
            )
            if state is not None:
                old_tops, old_totals, old_mixed = state[pair]
                scale = [jnp.exp(old_tops[half] - tops[half]) for half in range(2)]
                totals = [totals[half] + scale[half] * old_totals[half] for half in range(2)]
                mixed = mixed + old_mixed * jnp.where(low, scale[0], scale[1])
            found.append((tops, totals, mixed))
        return found

    keys_values(normed, tok)
    state = attend(tok, lines_of(tok), own_seg == seg_of(tok), None)
    for d in toks:
        who = lax.rem(tok + n_tok - d, n_tok)
        lines = lines_of(who)
        same = own_seg == seg_of(who)
        if d == 1:
            @at_end
            def _():
                push(n_in, n_in - 1)

        hid_copies[d - 1].wait_recv()
        keys_values(rms_scale(hid[who].astype(jnp.float32), g1[...]).astype(jnp.bfloat16), who)
        if d == 1:
            for load in loads[6:9]:
                load.wait()
            @at_end
            def _():
                share(0)
                push(n_in + 1, n_in)

        state = attend(who, lines, same, state)
    for pair, (_, totals, mixed) in enumerate(state):
        at = pair * 2 * HD
        att_scr[:, at:at + 2 * HD] = (mixed / jnp.where(low, totals[0], totals[1])).astype(
            jnp.bfloat16
        )
    for p in range(1, n_in):
        at_end(functools.partial(share, p))
    middle = hid[tok].astype(jnp.float32) + jnp.dot(
        att_scr[...], wo[...], preferred_element_type=jnp.float32
    )
    mid[...] = middle
    gath[0] = rms_scale(middle, g2[...]).astype(jnp.bfloat16)

    ag_rows = rows // AG

    def rows_at(slot, h):
        return gath.at[slot, pl.ds(h * ag_rows, ag_rows)]

    def z_copy(h):
        return remote(rows_at(0, h), rows_at(WIDE, h), s_z.at[h], r_gath.at[WIDE, h], near_dev)

    def y_copy(d, h):
        slot = WIDE - d
        to = dev(z, beside(d), c)
        return remote(rows_at(0, h), rows_at(slot, h), s_y.at[d, h], r_gath.at[slot, h], to)

    def on_copy(d, h):
        if h in BY_Z:
            slot, to = WIDE + d, near_dev
            return remote(rows_at(d, h), rows_at(slot, h), s_on.at[d, h], r_gath.at[slot, h], to)
        slot, to = slots - d, dev(z, beside(d), c)
        return remote(rows_at(WIDE, h), rows_at(slot, h), s_on.at[d, h], r_gath.at[slot, h], to)

    def arrived(slot, h):
        remote(
            rows_at(slot, h), rows_at(slot, h), s_z.at[h], r_gath.at[slot, h], core_dev
        ).wait_recv()

    def first(lo, n, k, n_k):
        inner = lax.dot_general(
            gath[lo:lo + n].reshape(n * rows, D), win[k:k + n_k].reshape(n_k * units, D),
            (((1,), (1,)), ((), ())), preferred_element_type=jnp.float32,
        )
        inner_scr[lo * rows:(lo + n) * rows, k * units:(k + n_k) * units] = jnp.maximum(
            inner, 0.0
        ).astype(jnp.bfloat16)

    def second(j):
        at = slice(j * cols, (j + 1) * cols)
        split = WIDE + 1
        weights = wout[j].reshape(4 * units, cols)
        terms = jnp.dot(inner_scr[split * rows:], weights, preferred_element_type=jnp.float32)
        part[j, split:] = terms.astype(jnp.bfloat16).reshape(WIDE - 1, rows, cols)
        for d in sides:
            corner_sum(d, j).start()
        terms = jnp.dot(inner_scr[:split * rows], weights, preferred_element_type=jnp.float32)
        mid[:, at] = mid[:, at] + terms[:rows]
        part[j, 1:split] = terms[rows:].astype(jnp.bfloat16).reshape(WIDE, rows, cols)

    def send_sum(kind, d, slot, j, to):
        return remote(
            part.at[j, slot], inbox.at[kind, d, j], s_out.at[kind, d, j], r_in.at[kind, d, j], to
        )

    def corner_sum(d, j):
        to = dev(z, beside(d), c) if j % 2 == 0 else near_dev
        return send_sum(0, d, WIDE + d, j, to)

    def side_sum(d, j):
        return send_sum(1, d, d, j, dev(z, beside(d), c))

    def near_sum(j):
        return send_sum(2, 0, WIDE, j, near_dev)

    def got(kind, d, j):
        send_sum(kind, d, 0, j, core_dev).wait_recv()
        return inbox[kind, d, j].astype(jnp.float32)

    def send(j):
        if j % 2 == 0:
            for d in sides:
                side_sum(d, j).start()
        else:
            near_sum(j).start()

    def merge(j):
        if j % 2 == 0:
            extra = got(0, 1, j)
            for d in sides[1:]:
                extra = extra + got(0, d, j)
            part[j, WIDE] = (part[j, WIDE].astype(jnp.float32) + extra).astype(jnp.bfloat16)
            near_sum(j).start()
        else:
            for d in sides:
                part[j, d] = (part[j, d].astype(jnp.float32) + got(0, d, j)).astype(jnp.bfloat16)
                side_sum(d, j).start()

    for h in range(AG):
        z_copy(h).start()
        for d in sides:
            y_copy(d, h).start()
    w0, w1, w2, w3 = range(n_in, n_piece)

    pair_copy(0).wait_recv()
    first(0, 1, 0, 2)
    @inside
    def _():
        push(w0, n_in - 1)
        far_copy(w1).start()
        for p in range(n_in):
            share(p)

    at_end(lambda: share(w0))

    def pass_on(h):
        if h in BY_Z:
            for d in sides:
                arrived(d, h)
                on_copy(d, h).start()
        else:
            arrived(WIDE, h)
            for d in sides:
                on_copy(d, h).start()

    for h in range(AG // 2):
        pass_on(h)

    @at_end
    def _():
        for p in range(n_in):
            hand(p)

    for h in range(AG // 2, AG):
        pass_on(h)

    @inside
    def _():
        push(w2, w0)
        push(w3, w1)
        share(w0)
        share(w1)

    @at_end
    def _():
        share(w1)
        push(w2, w1)
        far_copy(w3).start()

    @inside
    def _():
        for p in range(n_in):
            hand(p)

    for h in range(AG):
        if h in BY_Z:
            arrived(WIDE, h)
        else:
            for d in sides:
                arrived(d, h)
    first(1, WIDE, 0, 2)

    @inside
    def _():
        share(w2)
        share(w3)

    for p in range(n_in):
        have(p)
    first(0, WIDE + 1, 2, 2)

    hand(w0)
    for d in sides:
        for h in range(AG):
            arrived(WIDE + d, h)
    first(WIDE + 1, WIDE - 1, 0, 4)
    for k in range(CUT):
        pair_copy(k + 1).wait_recv()
    hand(w1)
    have(w0)
    second(0)
    send(0)

    @at_end
    def _():
        share(w2)
        share(w3)

    have(w1)
    second(1)
    send(1)
    hand(w2)
    merge(0)
    hand(w3)
    have(w2)
    second(2)
    send(2)
    merge(1)
    have(w3)
    second(3)
    send(3)
    merge(2)
    merge(3)
    for j in range(CUT):
        at = slice(j * cols, (j + 1) * cols)
        total = mid[:, at]
        for d in sides:
            total = total + got(1, d, j)
        total = total + got(2, 0, j)
        out_ref[:, at] = total.astype(jnp.bfloat16)

    for copy in hid_copies:
        copy.wait_send()
    for k in range(1 + CUT):
        pair_copy(k).wait_send()
    for p in (*range(n_in - 1), w2, w3):
        far_copy(p).wait_send()
    for p in range(n_piece):
        for d in toks:
            relay(p, d).wait_send()
        for d in range(n_tok):
            hand_copy(p, d).wait_send()
    for h in range(AG):
        z_copy(h).wait_send()
        for d in sides:
            y_copy(d, h).wait_send()
            on_copy(d, h).wait_send()
    for j in range(CUT):
        for d in sides:
            corner_sum(d, j).wait_send()
            side_sum(d, j).wait_send()
        near_sum(j).wait_send()


def per_device(
    n_tok, n_blk, hidden_in, seg_ids, norm_gain1, w_query, w_key_value, rel_bias, w_attn_out,
    norm_gain2, w_in, w_out,
):
    rows = hidden_in.shape[1]
    count = n_tok * rows
    units = w_in.shape[0]
    wide = n_blk // 8
    chips = 2 * wide
    cols = D // CUT
    dma = pltpu.SemaphoreType.DMA

    def half(*shape):
        return pltpu.VMEM(shape, jnp.bfloat16)

    def full(*shape):
        return pltpu.VMEM(shape, jnp.float32)

    out = pl.pallas_call(
        functools.partial(layer_kernel, wide),
        out_shape=jax.ShapeDtypeStruct((rows, D), jnp.bfloat16),
        in_specs=[HBM] * 10,
        out_specs=VM,
        scratch_shapes=[
            pltpu.VMEM((1, count), jnp.int32),
            full(1, D),
            full(HEADS, BUCKETS),
            full(1, D),
            half(D, D),
            half(D, 2 * D),
            half(D, D),
            half(4, units, D),
            half(CUT, 4, units, cols),
            half(n_tok, rows, D),
            half(rows, D),
            half(count, 2 * D),
            half(rows, D),
            full(rows, D),
            half(chips, rows, D),
            half(CUT, chips, rows, cols),
            half(3, wide, CUT, rows, cols),
            half(chips * rows, 4 * units),
            dma((9 + CUT,)),
            dma((n_tok,)),
            dma((n_tok,)),
            dma((1 + CUT,)),
            dma((1 + CUT,)),
            dma((2 + CUT,)),
            dma((2 + CUT, n_tok)),
            dma((2 + CUT, n_tok)),
            dma((2 + CUT, n_tok)),
            dma((2 + CUT, n_tok)),
            dma((AG,)),
            dma((wide, AG)),
            dma((wide, AG)),
            dma((chips, AG)),
            dma((3, wide, CUT)),
            dma((3, wide, CUT)),
        ],
        compiler_params=pltpu.CompilerParams(
            collective_id=0, has_side_effects=True, vmem_limit_bytes=48 << 20
        ),
    )(
        *[
            pltpu.with_memory_space_constraint(operand, pltpu.HBM)
            for operand in (
                hidden_in[0], seg_ids, norm_gain1[None], jnp.transpose(rel_bias),
                norm_gain2[None], w_query, w_key_value, w_attn_out, w_in, w_out,
            )
        ]
    )
    return out[None]


def solution(mesh):
    placed = (
        P("blk", "tok", None),
        P("blk", None),
        P(),
        P(),
        P(),
        P(),
        P(),
        P(),
        P("blk", None),
        P("blk", None),
    )
    return jax.shard_map(
        functools.partial(per_device, mesh.shape["tok"], mesh.shape["blk"]),
        mesh=mesh, in_specs=placed, out_specs=P("blk", "tok", None), check_vma=False,
    )
```
